256 devices in a mesh: row: 8 (over x, core), col: 32 (over y, z).
Axes of the slice: x: 4, y: 4, z: 8, core: 2. Of those that a mesh axis runs over, the one named last changes fastest.
Arguments:
- inv_diag: float32 [2, 2048, 2048], P(None, 'row', 'col'), may hold values from -1 to 2, as said below
- coupling: float32 [2048, 2048], P('row', 'col'), may hold values from -0.125 to 0.125
- top_rhs: float32 [2, 2048, 4096], P(None, 'row', 'col'), may hold values from -6 to 6
- panel: float32 [2, 8192, 2048], P(None, 'row', 'col'), may hold values from -0.125 to 0.125
- rhs: float32 [8192, 4096], P('row', 'col'), may hold values from -6 to 6
Outputs:
- solved: float32 [2, 2048, 4096], P(None, 'row', 'col')
- trailing: float32 [8192, 4096], P('row', 'col')
The draws below stay inside these ranges and needn't reach their ends.
Inputs may be any that keep to these rules, and one draw needn't show every extreme that they name: `inv_diag`: each of the two blocks is lower triangular with its diagonal in 1 to 2.
All inputs are finite; a program needn't handle non-finite values.
Results may differ from the reference program's by a relative error of at most 0.000073.
Values sent between devices are 32-bit elements; how exact they have to be, the bound alone decides.
A program may use at most 64 MiB of HBM per device.

```python
import jax
import jax.numpy as jnp
from jax import lax

NB = 2048
M = 8192
TIME = 4096


def draw_inv_diag(key, part):
    shape = (2, NB, NB)
    rowpos = lax.broadcasted_iota(jnp.int32, shape, 1)
    colpos = lax.broadcasted_iota(jnp.int32, shape, 2)
    key_off, key_diag = jax.random.split(key)
    below = jnp.clip(jax.random.normal(key_off, shape, jnp.float32) / NB ** 0.5, -0.5, 0.5)
    diagonal = jax.random.uniform(key_diag, shape, jnp.float32, 1.0, 2.0)
    value = jnp.where(rowpos > colpos, below, jnp.where(rowpos == colpos, diagonal, 0.0))
    value = jnp.where((rowpos == 1) & (colpos == 0), -1.0, value)
    value = jnp.where((rowpos == 0) & (colpos == 0), 2.0, value)
    return value.astype(jnp.float32)


def levels(key, extent, cuts, low, high):
    gain = 1.0
    for axis_at, shards_of in cuts:
        steps = jax.random.uniform(jax.random.fold_in(jax.random.fold_in(key, 6), axis_at), (shards_of,), jnp.float32, low / len(cuts), high / len(cuts))
        gain = gain * jnp.repeat(jnp.exp(steps), extent[axis_at] // shards_of).reshape((-1,) + (1,) * (len(extent) - 1 - axis_at))
    return gain


def noise(stream_key, extent, width, reach, pieces=(), held_as=jnp.bfloat16):
    array = jax.random.normal(stream_key, extent, jnp.float32) * width
    if len(pieces) > 0:
        array = levels(stream_key, extent, pieces, -0.22, 0.18) * array
    return jnp.clip(array, min=-reach, max=reach).astype(held_as)


def setup_inputs(seed: int = 0) -> dict:
    keys = jax.random.split(jax.random.key(seed), 6)
    return {
        "inv_diag": draw_inv_diag(jax.random.fold_in(keys[5], 71), 0),
        "coupling": noise(keys[1], (NB, NB), NB ** -0.5, 0.125, ((0, 8), (1, 32)), jnp.float32),
        "top_rhs": noise(keys[2], (2, NB, TIME), 1.0, 6.0, ((1, 8), (2, 32)), jnp.float32),
        "panel": noise(keys[3], (2, M, NB), NB ** -0.5, 0.125, ((1, 8), (2, 32)), jnp.float32),
        "rhs": noise(keys[4], (M, TIME), 1.0, 6.0, ((0, 8), (1, 32)), jnp.float32),
    }


def product(left, right):
    return jnp.dot(left, right, precision=lax.Precision.HIGHEST, preferred_element_type=jnp.float32)


def reference(inv_diag, coupling, top_rhs, panel, rhs):
    first = product(inv_diag[0], top_rhs[0])
    reduced = top_rhs[1] - product(coupling, first)
    second = product(inv_diag[1], reduced)
    solved = jnp.stack([first, second])
    trailing = rhs - (product(panel[0], first) + product(panel[1], second))
    return solved, trailing
```

```python
import jax
import jax.numpy as jnp
from jax import lax
from jax.experimental import pallas as pl
from jax.experimental.pallas import tpu as pltpu
from jax.sharding import PartitionSpec as P

MESH = pl.DeviceIdType.MESH
F32 = jnp.float32
BF16 = jnp.bfloat16
NX, NY, NZ = 4, 4, 8
KD, MD, TD = 64, 256, 128
HALF = KD // 2
CHUNKS = 4
N_COPIES = 200


def split(v):
    hi = v.astype(BF16)
    lo = (v - hi.astype(F32)).astype(BF16)
    return hi, lo


def dot(a, b):
    return jnp.dot(a, b, preferred_element_type=F32)


def dot3(hi, lo, w):
    wh, wl = split(w)
    return dot(hi, wh) + (dot(lo, wh) + dot(hi, wl))


def kernel(inv_h, cpl_h, top_h, pan_h, rhs_h, solved, trail,
           at, pt, xb, sb, rl, sh, part, r1, r2, top_v, rhs_v, send, recv, loc):
    row, col = lax.axis_index("row"), lax.axis_index("col")
    x, c = row // 2, row % 2
    y, z = col // NZ, col % NZ
    oc = 1 - c
    x_up, x_dn, x_op = (x + 1) % NX, (x + NX - 1) % NX, (x + 2) % NX
    y_up, y_dn, y_op = (y + 1) % NY, (y + NY - 1) % NY, (y + 2) % NY
    to_x_up, to_x_dn = (x_up * 2 + c, col), (x_dn * 2 + c, col)
    to_y_up, to_y_dn = (row, y_up * NZ + z), (row, y_dn * NZ + z)
    to_z_up, to_z_dn = (row, y * NZ + (z + 1) % NZ), (row, y * NZ + (z + NZ - 1) % NZ)
    to_core = (x * 2 + oc, col)

    sent = []

    class Copy:
        def __init__(self, src, dst, to, land):
            i = len(sent)
            sent.append(self)
            self.out = pltpu.make_async_remote_copy(
                src_ref=src, dst_ref=dst, send_sem=send.at[i], recv_sem=recv.at[i], device_id=to, device_id_type=MESH)
            self.into = pltpu.make_async_remote_copy(
                src_ref=land, dst_ref=land, send_sem=send.at[i], recv_sem=recv.at[i], device_id=to, device_id_type=MESH)
            self.out.start()

        def got(self):
            self.into.wait_recv()

    class ZRing:
        def __init__(self, view):
            self.view, self.step, self.live = view, 0, None

        def start(self):
            s = self.step
            up, dn = (z + NZ - s) % NZ, (z + s) % NZ
            l_up, l_dn = (z + 2 * NZ - 1 - s) % NZ, (z + 1 + s) % NZ
            a, b = self.view(up, 0), self.view(dn, 1)
            self.live = (Copy(a, a, to_z_up, self.view(l_up, 0)), Copy(b, b, to_z_dn, self.view(l_dn, 1)))

        def advance(self):
            for copy in self.live:
                copy.got()
            self.step += 1
            if self.step < NZ - 1:
                self.start()
            return self.step == NZ - 1

    class YGather:
        def __init__(self, view):
            v = self.view = view
            self.up0 = Copy(v(y, 0), v(y, 0), to_y_up, v(y_dn, 0))
            self.dn1 = Copy(v(y, 1), v(y, 1), to_y_dn, v(y_up, 1))
            self.up1 = Copy(v(y, 1), v(y, 1), to_y_up, v(y_dn, 1))
            self.dn0 = Copy(v(y, 0), v(y, 0), to_y_dn, v(y_up, 0))

        def forward(self):
            v = self.view
            self.up0.got()
            self.f0 = Copy(v(y_dn, 0), v(y_dn, 0), to_y_up, v(y_op, 0))
            self.dn1.got()
            self.f1 = Copy(v(y_up, 1), v(y_up, 1), to_y_dn, v(y_op, 1))

        def finish(self):
            for copy in (self.up1, self.dn0, self.f0, self.f1):
                copy.got()

    class XGather:
        def __init__(self, b):
            self.b = b
            me, other = xb.at[b, row], xb.at[b, x * 2 + oc]
            up, dn = xb.at[b, x_up * 2 + c], xb.at[b, x_dn * 2 + c]
            self.up = Copy(me, me, to_x_up, dn)
            self.dn = Copy(me, me, to_x_dn, up)
            self.own = Copy(me, me, to_core, other)

        def forward(self):
            b = self.b
            up, dn = xb.at[b, x_up * 2 + c], xb.at[b, x_dn * 2 + c]
            half = TD // 2
            self.up.got()
            s = xb.at[b, x_dn * 2 + c, pl.ds(0, half)]
            self.f0 = Copy(s, s, to_x_up, xb.at[b, x_op * 2 + c, pl.ds(0, half)])
            self.dn.got()
            s = xb.at[b, x_up * 2 + c, pl.ds(half, half)]
            self.f1 = Copy(s, s, to_x_dn, xb.at[b, x_op * 2 + c, pl.ds(half, half)])
            self.c0 = Copy(dn, dn, to_core, xb.at[b, x_dn * 2 + oc])
            self.c1 = Copy(up, up, to_core, xb.at[b, x_up * 2 + oc])

        def finish(self):
            b = self.b
            self.f0.got()
            self.f1.got()
            s = xb.at[b, x_op * 2 + c]
            self.c2 = Copy(s, s, to_core, xb.at[b, x_op * 2 + oc])

        def close(self):
            for copy in (self.own, self.c0, self.c1, self.c2):
                copy.got()

    class YSwap:
        def __init__(self, k, b):
            self.k, self.b = k, b
            half = TD // 2
            op = y_op * 2 + c
            self.r0 = Copy(xb.at[b, op, pl.ds(0, half)], rl.at[k, 0], to_y_up, rl.at[k, 0])
            self.r1 = Copy(xb.at[b, op, pl.ds(half, half)], rl.at[k, 1], to_y_dn, rl.at[k, 1])
            self.up = Copy(xb.at[b, y_up * 2 + c], sb.at[k, c, y], to_y_up, sb.at[k, c, y_dn])
            self.dn = Copy(xb.at[b, y_dn * 2 + c], sb.at[k, c, y], to_y_dn, sb.at[k, c, y_up])

        def forward(self):
            k = self.k
            half = TD // 2
            self.r0.got()
            self.f0 = Copy(rl.at[k, 0], sb.at[k, c, y_dn, pl.ds(0, half)], to_y_up, sb.at[k, c, y_op, pl.ds(0, half)])
            self.r1.got()
            self.f1 = Copy(rl.at[k, 1], sb.at[k, c, y_up, pl.ds(half, half)], to_y_dn,
                           sb.at[k, c, y_op, pl.ds(half, half)])
            self.up.got()
            s = sb.at[k, c, y_dn]
            self.c0 = Copy(s, s, to_core, sb.at[k, oc, y_dn])
            self.dn.got()
            s = sb.at[k, c, y_up]
            self.c1 = Copy(s, s, to_core, sb.at[k, oc, y_up])

        def finish(self):
            k = self.k
            self.f0.got()
            self.f1.got()
            s = sb.at[k, c, y_op]
            self.c2 = Copy(s, s, to_core, sb.at[k, oc, y_op])
            for cc in range(2):
                hi, lo = split(xb[self.b, y * 2 + cc])
                sh[k, cc, 0, y] = hi
                sh[k, cc, 1, y] = lo
            for yy in (y_dn, y_up, y_op):
                hi, lo = split(sb[k, c, yy])
                sh[k, c, 0, yy] = hi
                sh[k, c, 1, yy] = lo
            for copy in (self.c0, self.c1, self.c2):
                copy.got()
            for yy in (y_dn, y_up, y_op):
                hi, lo = split(sb[k, oc, yy])
                sh[k, oc, 0, yy] = hi
                sh[k, oc, 1, yy] = lo

    def solve(a, b):
        total = jnp.zeros((TD, MD), F32)
        for r in range(2 * NX):
            hi, lo = split(xb[b, r])
            w = at[a, r // 2, (r % 2) * 4:(r % 2) * 4 + 4].reshape(MD, MD)
            total = total + dot3(hi, lo, w)
        return total

    def partial(j, k):
        total = jnp.zeros((NY * TD, MD), F32)
        for cc in range(2):
            w = pt[j, k, 4 * cc:4 * cc + 4].reshape(MD, MD)
            hi = sh[k, cc, 0].reshape(NY * TD, MD)
            lo = sh[k, cc, 1].reshape(NY * TD, MD)
            total = total + dot3(hi, lo, w)
        return total.reshape(NY, TD, MD)

    class YSum:
        def __init__(self, j):
            self.j = j
            half = TD // 2
            self.a0 = Copy(part.at[j, y_op, pl.ds(0, half)], r1.at[j, 0], to_y_up, r1.at[j, 0])
            self.a1 = Copy(part.at[j, y_op, pl.ds(half, half)], r1.at[j, 1], to_y_dn, r1.at[j, 1])

        def forward(self):
            j = self.j
            half = TD // 2
            self.a0.got()
            part[j, y_up, pl.ds(0, half)] = part[j, y_up, pl.ds(0, half)] + r1[j, 0]
            self.b0 = Copy(part.at[j, y_up], r2.at[j, 0], to_y_up, r2.at[j, 0])
            self.a1.got()
            part[j, y_dn, pl.ds(half, half)] = part[j, y_dn, pl.ds(half, half)] + r1[j, 1]
            self.b1 = Copy(part.at[j, y_dn], r2.at[j, 1], to_y_dn, r2.at[j, 1])

        def finish(self):
            j = self.j
            self.b0.got()
            self.b1.got()
            total = part[j, y] + (r2[j, 0] + r2[j, 1])
            rows = pl.ds(j * MD, MD)
            trail[rows] = rhs_v[rows] - total.T

    local = []

    def bring(src, dst):
        copy = pltpu.make_async_copy(src, dst, loc.at[len(local)])
        local.append(copy)
        copy.start()
        return copy

    bring(inv_h.at[0], at.at[0, y, z])
    bring(cpl_h, at.at[1, y, z])
    bring(inv_h.at[1], at.at[2, y, z])
    bring(top_h, top_v)
    for j in range(CHUNKS):
        bring(pan_h.at[:, :, pl.ds(j * MD, MD)], pt.at[j, :, z])
    bring(rhs_h, rhs_v)

    barrier = pltpu.get_barrier_semaphore()
    peers = (to_x_up, to_x_dn, to_y_up, to_y_dn, to_z_up, to_z_dn, to_core)
    for peer in peers:
        pl.semaphore_signal(barrier, inc=1, device_id=peer, device_id_type=MESH)
    pl.semaphore_wait(barrier, len(peers))

    local[0].wait()
    gather_a0 = YGather(lambda yy, h: at.at[0, yy, z, pl.ds(h * HALF, HALF)])
    local[1].wait()
    local[2].wait()
    ring_ca = ZRing(lambda zz, h: at.at[pl.ds(1, 2), y, zz, pl.ds(h * HALF, HALF)])
    ring_ca.start()
    local[3].wait()
    xb[0, row] = top_v[0].T
    gx0 = XGather(0)
    gather_a0.forward()
    ring_ca.advance()
    gather_a0.finish()
    ring_a0 = ZRing(lambda zz, h: at.at[0, :, zz, pl.ds(h * HALF, HALF)])
    ring_a0.start()
    gx0.forward()
    ring_ca.advance()
    ring_a0.advance()
    gx0.finish()
    ring_ca.advance()
    ring_ca.advance()
    ring_a0.advance()
    gx0.close()
    ring_ca.advance()
    ring_ca.advance()
    ring_a0.advance()
    ring_ca.advance()
    gather_c = YGather(lambda yy, h: at.at[1, yy, :, pl.ds(h * HALF, HALF)])
    ring_a0.advance()
    ring_a0.advance()
    gather_c.forward()
    gather_a1 = YGather(lambda yy, h: at.at[2, yy, :, pl.ds(h * HALF, HALF)])
    for copy in local[4:]:
        copy.wait()
    rings = [ZRing(lambda zz, h, j=j: pt.at[j, :, zz, pl.ds(h * HALF, HALF)]) for j in range(CHUNKS)]
    rings[0].start()
    ring_a0.advance()
    rings[1].start()
    ring_a0.advance()

    def service(pair):
        rings[2 * pair].advance()
        return rings[2 * pair + 1].advance()

    first = solve(0, 0)
    xb[1, row] = first
    gx1 = XGather(1)
    solved[0] = first.T
    service(0)
    gather_c.finish()
    gx1.forward()
    service(0)
    gx1.finish()
    gx1.close()
    service(0)
    reduced = top_v[1].T - solve(1, 1)
    xb[2, row] = reduced
    gx2 = XGather(2)
    gather_a1.forward()
    service(0)
    gx2.forward()
    swap0 = YSwap(0, 1)
    service(0)
    gx2.finish()
    gather_a1.finish()
    gx2.close()
    service(0)
    second = solve(2, 2)
    xb[3, row] = second
    gx3 = XGather(3)
    solved[1] = second.T
    service(0)
    rings[2].start()
    rings[3].start()
    gx3.forward()
    swap0.forward()
    swap0.finish()
    for j in (0, 1):
        part[j] = partial(j, 0)
    gx3.finish()
    service(1)
    gx3.close()
    swap1 = YSwap(1, 3)
    service(1)
    swap1.forward()
    service(1)
    swap1.finish()
    sums = []
    for j in (0, 1):
        part[j] = part[j] + partial(j, 1)
        sums.append(YSum(j))
        service(1)
    sums[0].forward()
    service(1)
    sums[1].forward()
    service(1)
    for j in (2, 3):
        part[j] = partial(j, 0) + partial(j, 1)
        sums.append(YSum(j))
    for s in sums[2:]:
        s.forward()
    for s in sums:
        s.finish()
    for copy in sent:
        copy.out.wait_send()


def body(inv_diag, coupling, top_rhs, panel, rhs):
    hbm = pl.BlockSpec(memory_space=pl.ANY)
    vmem = pl.BlockSpec(memory_space=pltpu.VMEM)
    solved, trailing = pl.pallas_call(
        kernel,
        out_shape=(jax.ShapeDtypeStruct((2, MD, TD), F32), jax.ShapeDtypeStruct((CHUNKS * MD, TD), F32)),
        in_specs=[hbm] * 5,
        out_specs=(vmem, vmem),
        scratch_shapes=[
            pltpu.VMEM((3, NY, NZ, KD, MD), F32),
            pltpu.VMEM((CHUNKS, 2, NZ, KD, MD), F32),
            pltpu.VMEM((4, 2 * NX, TD, MD), F32),
            pltpu.VMEM((2, 2, NY, TD, MD), F32),
            pltpu.VMEM((2, 2, TD // 2, MD), F32),
            pltpu.VMEM((2, 2, 2, NY, TD, MD), BF16),
            pltpu.VMEM((CHUNKS, NY, TD, MD), F32),
            pltpu.VMEM((CHUNKS, 2, TD // 2, MD), F32),
            pltpu.VMEM((CHUNKS, 2, TD, MD), F32),
            pltpu.VMEM((2, MD, TD), F32),
            pltpu.VMEM((CHUNKS * MD, TD), F32),
            pltpu.SemaphoreType.DMA((N_COPIES,)),
            pltpu.SemaphoreType.DMA((N_COPIES,)),
            pltpu.SemaphoreType.DMA((16,)),
        ],
        compiler_params=pltpu.CompilerParams(
            collective_id=0, has_side_effects=True, vmem_limit_bytes=48 * 1024 * 1024),
    )(jnp.swapaxes(inv_diag, 1, 2), coupling.T, top_rhs, jnp.swapaxes(panel, 1, 2), rhs)
    return solved, trailing


def solution(mesh):
    in_specs = (
        P(None, "row", "col"),
        P("row", "col"),
        P(None, "row", "col"),
        P(None, "row", "col"),
        P("row", "col"),
    )
    out_specs = (P(None, "row", "col"), P("row", "col"))
    return jax.shard_map(body, mesh=mesh, in_specs=in_specs, out_specs=out_specs, check_vma=False)
```

```python
import jax
import jax.numpy as jnp
from jax import lax
from jax.experimental import pallas as pl
from jax.experimental.pallas import tpu as pltpu
from jax.sharding import PartitionSpec as P

MESH = pl.DeviceIdType.MESH
F32 = jnp.float32
BF16 = jnp.bfloat16
NX, NY, NZ = 4, 4, 8
KD, MD, TD = 64, 256, 128
KH, TH = KD // 2, TD // 2
CHUNKS = 4
N_COPIES = 240


def split(v):
    hi = v.astype(BF16)
    lo = (v - hi.astype(F32)).astype(BF16)
    return hi, lo


def dot(a, b):
    return jnp.dot(a, b, preferred_element_type=F32)


def dot3(hi, lo, w):
    wh, wl = split(w)
    return dot(hi, wh) + (dot(lo, wh) + dot(hi, wl))


def kernel(inv_h, cpl_h, top_h, pan_h, rhs_h, solved, trail,
           az, a1, pt, xm, sb, sh, xr, part, r1, r2, top_v, rhs_v, send, recv, arrive, loc):
    row, col = lax.axis_index("row"), lax.axis_index("col")
    x, c = row // 2, row % 2
    y, z = col // NZ, col % NZ
    oc = 1 - c
    x_up, x_dn, x_op = (x + 1) % NX, (x + NX - 1) % NX, (x + 2) % NX
    y_up, y_dn, y_op = (y + 1) % NY, (y + NY - 1) % NY, (y + 2) % NY
    to_x_up, to_x_dn = (x_up * 2 + c, col), (x_dn * 2 + c, col)
    to_y_up, to_y_dn, to_y_op = (row, y_up * NZ + z), (row, y_dn * NZ + z), (row, y_op * NZ + z)
    to_z_up, to_z_dn = (row, y * NZ + (z + 1) % NZ), (row, y * NZ + (z + NZ - 1) % NZ)
    to_core = (x * 2 + oc, col)
    halves = (pl.ds(0, TH), pl.ds(TH, TH))

    sent = []

    class Copy:
        def __init__(self, src, dst, to, land):
            i = len(sent)
            self.out = pltpu.make_async_remote_copy(
                src_ref=src, dst_ref=dst, send_sem=send.at[i], recv_sem=recv.at[i], device_id=to, device_id_type=MESH)
            self.into = pltpu.make_async_remote_copy(
                src_ref=land, dst_ref=land, send_sem=send.at[i], recv_sem=recv.at[i], device_id=to, device_id_type=MESH)
            sent.append((self.out, None))
            self.out.start()

        def got(self):
            self.into.wait_recv()

    def same(view, at, to, land):
        return Copy(view(at), view(at), to, view(land))

    class ZRing:
        def __init__(self, full, half):
            self.full, self.half, self.hop = full, half, 0

        def start(self):
            s = self.hop
            up, dn = (z + NZ - s) % NZ, (z + s) % NZ
            l_up, l_dn = (z + NZ - 1 - s) % NZ, (z + 1 + s) % NZ
            if s < 3:
                self.live = (same(self.full, up, to_z_up, l_up), same(self.full, dn, to_z_dn, l_dn))
            else:
                self.live = (same(lambda p: self.half(p, 0), up, to_z_up, l_up),
                             same(lambda p: self.half(p, 1), dn, to_z_dn, l_dn))

        def advance(self):
            for copy in self.live:
                copy.got()
            self.hop += 1
            if self.hop < 4:
                self.start()

    class YPiece:
        def __init__(self, zz):
            full = lambda p: a1.at[p, zz]
            self.zz = zz
            self.up = same(full, y, to_y_up, y_dn)
            self.dn = same(full, y, to_y_dn, y_up)

        def forward(self):
            lower = lambda p: a1.at[p, self.zz, pl.ds(0, KH)]
            upper = lambda p: a1.at[p, self.zz, pl.ds(KH, KH)]
            self.up.got()
            self.f0 = same(lower, y_dn, to_y_up, y_op)
            self.dn.got()
            self.f1 = same(upper, y_up, to_y_dn, y_op)

        def finish(self):
            self.f0.got()
            self.f1.got()

    class XGather:
        def __init__(self):
            whole = lambda p: xr.at[p]
            self.up = same(whole, row, to_x_up, x_dn * 2 + c)
            self.dn = same(whole, row, to_x_dn, x_up * 2 + c)
            self.own = same(whole, row, to_core, x * 2 + oc)

        def forward(self):
            whole = lambda p: xr.at[p]
            self.up.got()
            self.f0 = same(lambda p: xr.at[p, halves[0]], x_dn * 2 + c, to_x_up, x_op * 2 + c)
            self.dn.got()
            self.f1 = same(lambda p: xr.at[p, halves[1]], x_up * 2 + c, to_x_dn, x_op * 2 + c)
            self.c0 = same(whole, x_dn * 2 + c, to_core, x_dn * 2 + oc)
            self.c1 = same(whole, x_up * 2 + c, to_core, x_up * 2 + oc)

        def finish(self):
            self.f0.got()
            self.f1.got()
            self.c2 = same(lambda p: xr.at[p], x_op * 2 + c, to_core, x_op * 2 + oc)

        def close(self):
            for copy in (self.own, self.c0, self.c1, self.c2):
                copy.got()

    class Spread:
        def __init__(self, k):
            self.k = k
            lo, hi = self.part(0), self.part(1)
            self.u0 = same(lo, x, to_x_up, x_dn)
            self.d1 = same(hi, x, to_x_dn, x_up)
            self.u1 = same(hi, x, to_x_up, x_dn)
            self.d0 = same(lo, x, to_x_dn, x_up)
            self.turn(x, 0)
            self.turn(x, 1)

        def part(self, h):
            return lambda p: xm.at[self.k, p, halves[h]]

        def turn(self, xx, h):
            k = self.k
            behind = (y + NY - xx) % NY
            i = len(sent)

            def copy():
                return pltpu.make_async_remote_copy(
                    src_ref=xm.at[k, xx, halves[h]], dst_ref=sb.at[k, c, y, halves[h]], send_sem=send.at[i],
                    recv_sem=arrive.at[k, behind * 2 + h], device_id=(row, xx * NZ + z), device_id_type=MESH)

            sent.append((copy(), behind != 0))

            @pl.when(behind != 0)
            def _():
                copy().start()

        def hop1(self):
            lo, hi = self.part(0), self.part(1)
            self.u0.got()
            self.f0 = same(lo, x_dn, to_x_up, x_op)
            self.turn(x_dn, 0)
            self.d1.got()
            self.f1 = same(hi, x_up, to_x_dn, x_op)
            self.turn(x_up, 1)
            self.u1.got()
            self.turn(x_dn, 1)
            self.d0.got()
            self.turn(x_up, 0)

        def hop2(self):
            k = self.k
            self.f0.got()
            self.turn(x_op, 0)
            self.f1.got()
            self.turn(x_op, 1)
            self.cores = [Copy(xm.at[k, y], sb.at[k, c, y], to_core, sb.at[k, oc, y])]

        def arrived(self):
            k = self.k
            for behind, to in ((1, to_y_up), (3, to_y_dn), (2, to_y_op)):
                src = (y + behind) % NY
                for h in range(2):
                    land = sb.at[k, c, src, halves[h]]
                    pltpu.make_async_remote_copy(
                        src_ref=land, dst_ref=land, send_sem=send.at[0], recv_sem=arrive.at[k, behind * 2 + h],
                        device_id=to, device_id_type=MESH).wait_recv()
                self.cores.append(same(lambda p: sb.at[k, p, src], c, to_core, oc))
            self.keep(c, y, xm[k, y])
            for behind in (1, 3, 2):
                src = (y + behind) % NY
                self.keep(c, src, sb[k, c, src])

        def keep(self, cc, src, value):
            hi, lo = split(value)
            sh[self.k, cc, 0, src] = hi
            sh[self.k, cc, 1, src] = lo

        def finish(self):
            for copy in self.cores:
                copy.got()
            for src in range(NY):
                self.keep(oc, src, sb[self.k, oc, src])

    def solve():
        total = jnp.zeros((TD, MD), F32)
        for r in range(2 * NX):
            hi, lo = split(xr[r])
            w = a1[r // 2, (r % 2) * 4:(r % 2) * 4 + 4].reshape(MD, MD)
            total = total + dot3(hi, lo, w)
        return total

    def partial(k, weight):
        total = jnp.zeros((NY * TD, MD), F32)
        for cc in range(2):
            hi = sh[k, cc, 0].reshape(NY * TD, MD)
            lo = sh[k, cc, 1].reshape(NY * TD, MD)
            total = total + dot3(hi, lo, weight(cc).reshape(MD, MD))
        return total.reshape(NY, TD, MD)

    def factor(i):
        return lambda cc: az[i, 4 * cc:4 * cc + 4]

    def panel(j, k):
        return lambda cc: pt[j, k, 4 * cc:4 * cc + 4]

    class YSum:
        def __init__(self, j):
            self.j = j
            self.a0 = Copy(part.at[j, y_op, halves[0]], r1.at[j, 0], to_y_up, r1.at[j, 0])
            self.a1 = Copy(part.at[j, y_op, halves[1]], r1.at[j, 1], to_y_dn, r1.at[j, 1])

        def forward(self):
            j = self.j
            self.a0.got()
            part[j, y_up, halves[0]] = part[j, y_up, halves[0]] + r1[j, 0]
            self.b0 = Copy(part.at[j, y_up], r2.at[j, 0], to_y_up, r2.at[j, 0])
            self.a1.got()
            part[j, y_dn, halves[1]] = part[j, y_dn, halves[1]] + r1[j, 1]
            self.b1 = Copy(part.at[j, y_dn], r2.at[j, 1], to_y_dn, r2.at[j, 1])

        def total(self):
            j = self.j
            self.b0.got()
            self.b1.got()
            return part[j, y] + (r2[j, 0] + r2[j, 1])

        def store(self):
            rows = pl.ds(self.j * MD, MD)
            trail[rows] = rhs_v[rows] - self.total().T

    local = []

    def bring(src, dst):
        copy = pltpu.make_async_copy(src, dst, loc.at[len(local)])
        local.append(copy)
        copy.start()

    bring(top_h, top_v)
    bring(inv_h.at[0], az.at[0, z])
    bring(cpl_h, az.at[1, z])
    bring(inv_h.at[1], a1.at[y, z])
    for j in range(CHUNKS):
        bring(pan_h.at[:, :, pl.ds(j * MD, MD)], pt.at[j, :, z])
    bring(rhs_h, rhs_v)

    barrier = pltpu.get_barrier_semaphore()
    peers = (to_x_up, to_x_dn, to_y_up, to_y_dn, to_y_op, to_z_up, to_z_dn, to_core)
    for peer in peers:
        pl.semaphore_signal(barrier, inc=1, device_id=peer, device_id_type=MESH)
    local[0].wait()
    xm[0, x] = top_v[0].T
    for copy in local[1:4]:
        copy.wait()
    pl.semaphore_wait(barrier, len(peers))

    spread0 = Spread(0)
    ring0 = ZRing(lambda p: az.at[0, p], lambda p, h: az.at[0, p, pl.ds(h * KH, KH)])
    ring1 = ZRing(lambda p: az.at[1, p], lambda p, h: az.at[1, p, pl.ds(h * KH, KH)])
    ring2 = ZRing(lambda p: a1.at[y, p], lambda p, h: a1.at[y, p, pl.ds(h * KH, KH)])
    rings = [ZRing(lambda p, j=j: pt.at[j, :, p], lambda p, h, j=j: pt.at[j, :, p, pl.ds(h * KH, KH)])
             for j in range(CHUNKS)]

    def at_z(d):
        return (z + NZ + d) % NZ

    ring0.start()
    ring1.start()
    ring2.start()
    pieces = [YPiece(z)]
    spread0.hop1()
    ring0.advance()
    ring1.advance()
    ring2.advance()
    pieces += [YPiece(at_z(-1))]
    spread0.hop2()
    ring0.advance()
    ring1.advance()
    ring2.advance()
    pieces += [YPiece(at_z(1))]
    spread0.arrived()
    ring0.advance()
    ring1.advance()
    ring2.advance()
    for copy in local[4:]:
        copy.wait()
    rings[0].start()
    rings[1].start()
    spread0.finish()
    ring0.advance()

    part[4] = partial(0, factor(0))
    sum4 = YSum(4)
    for piece in pieces:
        piece.forward()
    ring1.advance()
    ring2.advance()
    sum4.forward()
    pieces += [YPiece(at_z(d)) for d in (-2, 2)]
    rings[0].advance()
    first = sum4.total()
    xm[1, x] = first
    spread1 = Spread(1)
    solved[0] = first.T
    rings[1].advance()
    pieces[3].forward()
    pieces[4].forward()
    spread1.hop1()
    rings[0].advance()
    spread1.hop2()
    rings[1].advance()
    spread1.arrived()
    rings[0].advance()
    spread1.finish()

    part[5] = partial(1, factor(1))
    sum5 = YSum(5)
    pieces += [YPiece(at_z(d)) for d in (-3, 3, 4)]
    rings[1].advance()
    sum5.forward()
    for piece in pieces[5:]:
        piece.forward()
    rings[0].advance()
    rings[2].start()
    rings[1].advance()
    rings[3].start()
    reduced = top_v[1].T - sum5.total()
    xr[row] = reduced
    gather = XGather()
    for j in (0, 1):
        part[j] = partial(1, panel(j, 0))
    gather.forward()
    rings[2].advance()
    gather.finish()
    for piece in pieces:
        piece.finish()
    rings[3].advance()
    gather.close()
    second = solve()
    xm[2, x] = second
    spread2 = Spread(2)
    solved[1] = second.T
    rings[2].advance()
    spread2.hop1()
    rings[3].advance()
    spread2.hop2()
    rings[2].advance()
    rings[3].advance()
    spread2.arrived()
    rings[2].advance()
    spread2.finish()
    sums = []
    for j in (0, 1):
        part[j] = part[j] + partial(2, panel(j, 1))
        sums.append(YSum(j))
    rings[3].advance()
    sums[0].forward()
    part[2] = partial(1, panel(2, 0)) + partial(2, panel(2, 1))
    sums.append(YSum(2))
    sums[1].forward()
    part[3] = partial(1, panel(3, 0)) + partial(2, panel(3, 1))
    sums.append(YSum(3))
    sums[2].forward()
    sums[3].forward()
    for s in sums:
        s.store()
    for copy, when in sent:
        if when is None:
            copy.wait_send()
        else:
            pl.when(when)(copy.wait_send)


def body(inv_diag, coupling, top_rhs, panel, rhs):
    hbm = pl.BlockSpec(memory_space=pltpu.HBM)
    vmem = pl.BlockSpec(memory_space=pltpu.VMEM)
    solved, trailing = pl.pallas_call(
        kernel,
        out_shape=(jax.ShapeDtypeStruct((2, MD, TD), F32), jax.ShapeDtypeStruct((CHUNKS * MD, TD), F32)),
        in_specs=[hbm] * 5,
        out_specs=(vmem, vmem),
        scratch_shapes=[
            pltpu.VMEM((2, NZ, KD, MD), F32),
            pltpu.VMEM((NY, NZ, KD, MD), F32),
            pltpu.VMEM((CHUNKS, 2, NZ, KD, MD), F32),
            pltpu.VMEM((3, NX, TD, MD), F32),
            pltpu.VMEM((3, 2, NY, TD, MD), F32),
            pltpu.VMEM((3, 2, 2, NY, TD, MD), BF16),
            pltpu.VMEM((2 * NX, TD, MD), F32),
            pltpu.VMEM((CHUNKS + 2, NY, TD, MD), F32),
            pltpu.VMEM((CHUNKS + 2, 2, TH, MD), F32),
            pltpu.VMEM((CHUNKS + 2, 2, TD, MD), F32),
            pltpu.VMEM((2, MD, TD), F32),
            pltpu.VMEM((CHUNKS * MD, TD), F32),
            pltpu.SemaphoreType.DMA((N_COPIES,)),
            pltpu.SemaphoreType.DMA((N_COPIES,)),
            pltpu.SemaphoreType.DMA((3, 2 * NY)),
            pltpu.SemaphoreType.DMA((16,)),
        ],
        compiler_params=pltpu.CompilerParams(
            collective_id=0, has_side_effects=True, vmem_limit_bytes=60 * 1024 * 1024),
    )(jnp.swapaxes(inv_diag, 1, 2), coupling.T, top_rhs, jnp.swapaxes(panel, 1, 2), rhs)
    return solved, trailing


def solution(mesh):
    in_specs = (
        P(None, "row", "col"),
        P("row", "col"),
        P(None, "row", "col"),
        P(None, "row", "col"),
        P("row", "col"),
    )
    out_specs = (P(None, "row", "col"), P("row", "col"))
    return jax.shard_map(body, mesh=mesh, in_specs=in_specs, out_specs=out_specs, check_vma=False)
```

```python
import jax
import jax.numpy as jnp
from jax import lax
from jax.experimental import pallas as pl
from jax.experimental.pallas import tpu as pltpu
from jax.sharding import PartitionSpec as P

MESH = pl.DeviceIdType.MESH
F32 = jnp.float32
BF16 = jnp.bfloat16
NX, NY, NZ = 4, 4, 8
KD, MD, TD = 64, 256, 128
KH = KD // 2
CHUNKS = 4
N_COPIES = 240


def split(v):
    hi = v.astype(BF16)
    lo = (v - hi.astype(F32)).astype(BF16)
    return hi, lo


def dot(a, b):
    return jnp.dot(a, b, preferred_element_type=F32)


def dot3(hi, lo, w):
    wh, wl = split(w)
    return dot(hi, wh) + (dot(lo, wh) + dot(hi, wl))


def kernel(inv_h, cpl_h, top_h, pan_h, rhs_h, solved, trail,
           az, pt, xs, sb, sh, part, rs, top_v, rhs_v, send, recv, arrive, loc):
    row, col = lax.axis_index("row"), lax.axis_index("col")
    x, c = row // 2, row % 2
    y, z = col // NZ, col % NZ
    oc = 1 - c
    x_up, x_dn, x_op = (x + 1) % NX, (x + NX - 1) % NX, (x + 2) % NX
    y_up, y_dn, y_op = (y + 1) % NY, (y + NY - 1) % NY, (y + 2) % NY
    to_x_up, to_x_dn = (x_up * 2 + c, col), (x_dn * 2 + c, col)
    to_y_up, to_y_dn, to_y_op = (row, y_up * NZ + z), (row, y_dn * NZ + z), (row, y_op * NZ + z)
    to_z_up, to_z_dn = (row, y * NZ + (z + 1) % NZ), (row, y * NZ + (z + NZ - 1) % NZ)
    to_x_op = (x_op * 2 + c, col)
    to_core = (x * 2 + oc, col)

    halves = (pl.ds(0, TD // 2), pl.ds(TD // 2, TD // 2))

    def at_z(d):
        return (z + NZ + d) % NZ

    sent = []

    class Copy:
        def __init__(self, src, dst, to, land):
            i = len(sent)
            self.out = pltpu.make_async_remote_copy(
                src_ref=src, dst_ref=dst, send_sem=send.at[i], recv_sem=recv.at[i], device_id=to, device_id_type=MESH)
            self.into = pltpu.make_async_remote_copy(
                src_ref=land, dst_ref=land, send_sem=send.at[i], recv_sem=recv.at[i], device_id=to, device_id_type=MESH)
            sent.append((self.out, None))
            self.out.start()

        def got(self):
            self.into.wait_recv()

    def same(view, at, to, land):
        return Copy(view(at), view(at), to, view(land))

    class ZRing:
        def __init__(self, full, half):
            self.full, self.half, self.hop = full, half, 0

        def start(self):
            s = self.hop
            up, dn = (z + NZ - s) % NZ, (z + s) % NZ
            l_up, l_dn = (z + NZ - 1 - s) % NZ, (z + 1 + s) % NZ
            if s < 3:
                self.live = (same(self.full, up, to_z_up, l_up), same(self.full, dn, to_z_dn, l_dn))
            else:
                self.live = (same(lambda p: self.half(p, 0), up, to_z_up, l_up),
                             same(lambda p: self.half(p, 1), dn, to_z_dn, l_dn))

        def advance(self):
            for copy in self.live:
                copy.got()
            self.hop += 1
            if self.hop < 4:
                self.start()

    class ZPair:
        def __init__(self, full, half):
            self.full, self.half = full, half
            self.near = [same(full, z, (row, y * NZ + at_z(d)), at_z(-d)) for d in (2, -2, 1, -1)]

        def forward(self):
            far_up, far_dn = (row, y * NZ + at_z(2)), (row, y * NZ + at_z(-2))
            for copy in self.near[2:]:
                copy.got()
            self.far = [same(self.full, at_z(-1), far_up, at_z(-3)), same(self.full, at_z(1), far_dn, at_z(3))]
            for copy in self.near[:2]:
                copy.got()
            self.far += [same(lambda p: self.half(p, 0), at_z(-2), far_up, at_z(4)),
                         same(lambda p: self.half(p, 1), at_z(2), far_dn, at_z(4))]

        def finish(self):
            for copy in self.far:
                copy.got()

    class Inbox:
        def __init__(self, k):
            self.k, self.cores = k, []

        def post(self, src, to, behind, when=None):
            k, i = self.k, len(sent)

            def copy():
                return pltpu.make_async_remote_copy(
                    src_ref=src, dst_ref=sb.at[k, c, y], send_sem=send.at[i], recv_sem=arrive.at[k, behind],
                    device_id=to, device_id_type=MESH)

            sent.append((copy(), when))
            if when is None:
                copy().start()
            else:
                @pl.when(when)
                def _():
                    copy().start()

        def take(self, behind, when=None):
            k = self.k
            src = (y + behind) % NY
            land = sb.at[k, c, src]

            def wait():
                pltpu.make_async_remote_copy(
                    src_ref=land, dst_ref=land, send_sem=send.at[0], recv_sem=arrive.at[k, behind],
                    device_id=to_core, device_id_type=MESH).wait_recv()

            if when is None:
                wait()
            else:
                pl.when(when)(wait)
            self.share(src)

        def share(self, src):
            self.cores.append(same(lambda p: sb.at[self.k, p, src], c, to_core, oc))

        def keep(self, cc):
            for src in range(NY):
                hi, lo = split(sb[self.k, cc, src])
                sh[self.k, cc, 0, src] = hi
                sh[self.k, cc, 1, src] = lo

        def finish(self):
            self.keep(c)
            for copy in self.cores:
                copy.got()
            self.keep(oc)

    class Spread(Inbox):
        def __init__(self, k):
            super().__init__(k)
            behind = (y + NY - x) % NY
            for xx in (x_op, x_up, x_dn):
                self.post(xs.at[k], (xx * 2 + c, x * NZ + z), behind)
            self.post(xs.at[k], (row, x * NZ + z), behind, x != y)

            @pl.when(x == y)
            def _():
                sb[k, c, y] = xs[k]

        def arrived(self):
            for behind in (1, 3, 2):
                self.take(behind)
            self.take(0, x != y)

    def partial(k, weight):
        total = jnp.zeros((NY * TD, MD), F32)
        for cc in range(2):
            hi = sh[k, cc, 0].reshape(NY * TD, MD)
            lo = sh[k, cc, 1].reshape(NY * TD, MD)
            total = total + dot3(hi, lo, weight(cc).reshape(MD, MD))
        return total.reshape(NY, TD, MD)

    def panel(j, k):
        return lambda cc: pt[j, k, 4 * cc:4 * cc + 4]

    class YSum:
        def __init__(self, j):
            self.j = j
            self.live = [Copy(part.at[j, yy], rs.at[j, n], to, rs.at[j, n]) for n, (yy, to) in
                         enumerate(((y_op, to_y_op), (y_up, to_y_up), (y_dn, to_y_dn)))]

        def total(self):
            j = self.j
            for copy in self.live:
                copy.got()
            return (part[j, y] + rs[j, 0]) + (rs[j, 1] + rs[j, 2])

    class YRelay:
        def __init__(self, j):
            self.j = j
            self.a0 = Copy(part.at[j, y_op, halves[0]], rs.at[j, 2, halves[0]], to_y_up, rs.at[j, 2, halves[0]])
            self.a1 = Copy(part.at[j, y_op, halves[1]], rs.at[j, 2, halves[1]], to_y_dn, rs.at[j, 2, halves[1]])
            self.live = [self.send(0, y_up, 1, to_y_up), self.send(1, y_dn, 0, to_y_dn)]

        def send(self, way, to, h, device):
            land = rs.at[self.j, way, halves[h]]
            return Copy(part.at[self.j, to, halves[h]], land, device, land)

        def forward(self):
            j = self.j
            self.a0.got()
            part[j, y_up, halves[0]] = part[j, y_up, halves[0]] + rs[j, 2, halves[0]]
            self.live.append(self.send(0, y_up, 0, to_y_up))
            self.a1.got()
            part[j, y_dn, halves[1]] = part[j, y_dn, halves[1]] + rs[j, 2, halves[1]]
            self.live.append(self.send(1, y_dn, 1, to_y_dn))

        def store(self):
            j = self.j
            for copy in self.live:
                copy.got()
            rows = pl.ds(j * MD, MD)
            trail[rows] = rhs_v[rows] - (part[j, y] + (rs[j, 0] + rs[j, 1])).T

    local = []

    def bring(src, dst):
        copy = pltpu.make_async_copy(src, dst, loc.at[len(local)])
        local.append(copy)
        copy.start()

    bring(top_h, top_v)
    bring(inv_h.at[0], az.at[0, z])
    bring(cpl_h, az.at[1, z])
    bring(inv_h.at[1], az.at[2, z])
    for j in range(CHUNKS):
        bring(pan_h.at[:, :, pl.ds(j * MD, MD)], pt.at[j, :, z])
    bring(rhs_h, rhs_v)

    barrier = pltpu.get_barrier_semaphore()
    peers = [(((x + dx) % NX) * 2 + c, ((y + dy) % NY) * NZ + z) for dx in range(NX) for dy in range(NY) if dx or dy]
    peers += [(row, y * NZ + at_z(d)) for d in range(1, NZ)] + [to_core]
    for peer in peers:
        pl.semaphore_signal(barrier, inc=1, device_id=peer, device_id_type=MESH)
    local[0].wait()
    xs[0] = top_v[0].T
    for copy in local[1:4]:
        copy.wait()
    pl.semaphore_wait(barrier, len(peers))

    views = lambda i: (lambda p: az.at[i, p], lambda p, h: az.at[i, p, pl.ds(h * KH, KH)])
    rings = [ZRing(lambda p, j=j: pt.at[j, :, p], lambda p, h, j=j: pt.at[j, :, p, pl.ds(h * KH, KH)])
             for j in range(CHUNKS)]
    factor = lambda i: lambda cc: az[i, 4 * cc:4 * cc + 4]

    spread0 = Spread(0)
    pair0 = ZPair(*views(0))
    ring_c, ring_a = ZRing(*views(1)), ZRing(*views(2))
    ring_c.start()
    pair0.forward()
    ring_c.advance()
    ring_a.start()
    for copy in local[4:]:
        copy.wait()
    spread0.arrived()
    spread0.finish()
    ring_c.advance()
    pair0.finish()
    part[4] = partial(0, factor(0))
    sum4 = YSum(4)
    ring_a.advance()
    rings[0].start()
    ring_c.advance()
    rings[1].start()
    ring_a.advance()
    first = sum4.total()
    xs[1] = first
    spread1 = Spread(1)
    solved[0] = first.T
    ring_c.advance()
    rings[0].advance()
    ring_a.advance()
    rings[1].advance()
    spread1.arrived()
    ring_a.advance()
    spread1.finish()
    part[5] = partial(1, factor(1))
    sum5 = YSum(5)
    rings[0].advance()
    rings[1].advance()
    reduced = top_v[1].T - sum5.total()
    xs[2] = reduced
    spread2 = Spread(2)
    rings[0].advance()
    rings[1].advance()
    spread2.arrived()
    rings[2].start()
    rings[3].start()
    spread2.finish()
    part[6] = partial(2, factor(2))
    sum6 = YSum(6)
    rings[0].advance()
    part[0] = partial(1, panel(0, 0))
    rings[1].advance()
    part[1] = partial(1, panel(1, 0))
    second = sum6.total()
    xs[3] = second
    spread3 = Spread(3)
    solved[1] = second.T
    rings[2].advance()
    rings[3].advance()
    spread3.arrived()
    rings[2].advance()
    rings[3].advance()
    spread3.finish()
    sums = []
    part[0] = part[0] + partial(3, panel(0, 1))
    sums.append(YRelay(0))
    part[1] = part[1] + partial(3, panel(1, 1))
    sums.append(YRelay(1))
    rings[2].advance()
    rings[3].advance()
    sums[0].forward()
    sums[1].forward()
    rings[2].advance()
    part[2] = partial(1, panel(2, 0)) + partial(3, panel(2, 1))
    sums.append(YRelay(2))
    rings[3].advance()
    part[3] = partial(1, panel(3, 0)) + partial(3, panel(3, 1))
    sums.append(YRelay(3))
    sums[2].forward()
    sums[3].forward()
    for s in sums:
        s.store()
    for copy, when in sent:
        if when is None:
            copy.wait_send()
        else:
            pl.when(when)(copy.wait_send)


def body(inv_diag, coupling, top_rhs, panel, rhs):
    hbm = pl.BlockSpec(memory_space=pltpu.HBM)
    vmem = pl.BlockSpec(memory_space=pltpu.VMEM)
    solved, trailing = pl.pallas_call(
        kernel,
        out_shape=(jax.ShapeDtypeStruct((2, MD, TD), F32), jax.ShapeDtypeStruct((CHUNKS * MD, TD), F32)),
        in_specs=[hbm] * 5,
        out_specs=(vmem, vmem),
        scratch_shapes=[
            pltpu.VMEM((3, NZ, KD, MD), F32),
            pltpu.VMEM((CHUNKS, 2, NZ, KD, MD), F32),
            pltpu.VMEM((4, TD, MD), F32),
            pltpu.VMEM((4, 2, NY, TD, MD), F32),
            pltpu.VMEM((4, 2, 2, NY, TD, MD), BF16),
            pltpu.VMEM((CHUNKS + 3, NY, TD, MD), F32),
            pltpu.VMEM((CHUNKS + 3, NY - 1, TD, MD), F32),
            pltpu.VMEM((2, MD, TD), F32),
            pltpu.VMEM((CHUNKS * MD, TD), F32),
            pltpu.SemaphoreType.DMA((N_COPIES,)),
            pltpu.SemaphoreType.DMA((N_COPIES,)),
            pltpu.SemaphoreType.DMA((4, NY)),
            pltpu.SemaphoreType.DMA((16,)),
        ],
        compiler_params=pltpu.CompilerParams(
            collective_id=0, has_side_effects=True, vmem_limit_bytes=62 * 1024 * 1024),
    )(jnp.swapaxes(inv_diag, 1, 2), coupling.T, top_rhs, jnp.swapaxes(panel, 1, 2), rhs)
    return solved, trailing


def solution(mesh):
    in_specs = (
        P(None, "row", "col"),
        P("row", "col"),
        P(None, "row", "col"),
        P(None, "row", "col"),
        P("row", "col"),
    )
    out_specs = (P(None, "row", "col"), P("row", "col"))
    return jax.shard_map(body, mesh=mesh, in_specs=in_specs, out_specs=out_specs, check_vma=False)
```

```python
import jax
import jax.numpy as jnp
from jax import lax
from jax.experimental import pallas as pl
from jax.experimental.pallas import tpu as pltpu
from jax.sharding import PartitionSpec as P

MESH = pl.DeviceIdType.MESH
F32 = jnp.float32
BF16 = jnp.bfloat16
NX, NY, NZ = 4, 4, 8
KD, MD, TD = 64, 256, 128
KH = KD // 2
CHUNKS = 4
N_SEND, N_RECV, N_LOCAL = 29, 46, 9


def split(v):
    hi = v.astype(BF16)
    lo = (v - hi.astype(F32)).astype(BF16)
    return hi, lo


def dot(a, b):
    return jnp.dot(a, b, preferred_element_type=F32)


def dot3(hi, lo, w):
    wh, wl = split(w)
    return dot(hi, wh) + (dot(lo, wh) + dot(hi, wl))


def kernel(inv_h, cpl_h, top_h, pan_h, rhs_h, solved, trail,
           az, pt, xs, sb, sh, cb, ch, xc, part, rs, wp, wr, top_v, rhs_v, send, recv, arrive, loc):
    row, col = lax.axis_index("row"), lax.axis_index("col")
    x, c = row // 2, row % 2
    y, z = col // NZ, col % NZ
    oc = 1 - c
    x_up, x_dn, x_op = (x + 1) % NX, (x + NX - 1) % NX, (x + 2) % NX
    y_up, y_dn, y_op = (y + 1) % NY, (y + NY - 1) % NY, (y + 2) % NY
    to_x_up, to_x_dn = (x_up * 2 + c, col), (x_dn * 2 + c, col)
    to_y_up, to_y_dn, to_y_op = (row, y_up * NZ + z), (row, y_dn * NZ + z), (row, y_op * NZ + z)
    to_z_up, to_z_dn = (row, y * NZ + (z + 1) % NZ), (row, y * NZ + (z + NZ - 1) % NZ)
    to_x_op = (x_op * 2 + c, col)
    to_core = (x * 2 + oc, col)

    halves = (pl.ds(0, TD // 2), pl.ds(TD // 2, TD // 2))

    def at_z(d):
        return (z + NZ + d) % NZ

    used = {"send": 0, "recv": 0}
    drains = []

    def fresh(kind):
        used[kind] += 1
        return used[kind] - 1

    def group(ref, when=None):
        s = fresh("send")
        drains.append((ref, s, when))
        return s

    def remote(src, dst, to, s, sem):
        return pltpu.make_async_remote_copy(
            src_ref=src, dst_ref=dst, send_sem=send.at[s], recv_sem=sem, device_id=to, device_id_type=MESH)

    def push(src, dst, to, s, r):
        remote(src, dst, to, s, recv.at[r]).start()

    def move(view, at, to, s, r):
        push(view(at), view(at), to, s, r)

    def got(ref, r):
        remote(ref, ref, to_core, 0, recv.at[r]).wait_recv()

    class ZRing:
        def __init__(self, full, half, run):
            self.full, self.half, self.run, self.hop, self.s = full, half, run, 0, group(run(7))

        def start(self):
            s = self.hop
            up, dn = (z + NZ - s) % NZ, (z + s) % NZ
            self.r = fresh("recv")
            for at, to, h in ((up, to_z_up, 0), (dn, to_z_dn, 1)):
                move(self.full if s < 3 else lambda p: self.half(p, h), at, to, self.s, self.r)

        def advance(self):
            got(self.run(2 if self.hop < 3 else 1), self.r)
            self.hop += 1
            if self.hop < 4:
                self.start()

    class ZPair:
        def __init__(self, full, half, run):
            self.full, self.half, self.run, self.s = full, half, run, group(run(7))
            self.r = [fresh("recv") for _ in range(3)]
            for d in (2, -2, 1, -1):
                move(full, z, (row, y * NZ + at_z(d)), self.s, self.r[abs(d) - 1])

        def forward(self):
            far_up, far_dn = (row, y * NZ + at_z(2)), (row, y * NZ + at_z(-2))
            got(self.run(2), self.r[0])
            move(self.full, at_z(-1), far_up, self.s, self.r[2])
            move(self.full, at_z(1), far_dn, self.s, self.r[2])
            got(self.run(2), self.r[1])
            move(lambda p: self.half(p, 0), at_z(-2), far_up, self.s, self.r[2])
            move(lambda p: self.half(p, 1), at_z(2), far_dn, self.s, self.r[2])

        def finish(self):
            got(self.run(3), self.r[2])

    class Spread:
        def __init__(self, k, src, box, kept):
            self.k, self.box, self.kept = k, box, kept
            self.s, self.r = group(box.at[0]), fresh("recv")
            behind = (y + NY - x) % NY
            here = group(src, x != y)
            there = group(box.at[0, pl.ds(0, 3)])
            for xx in (x_op, x_up, x_dn):
                self.post(src, (xx * 2 + c, x * NZ + z), behind, there).start()

            @pl.when(x != y)
            def _():
                self.post(src, (row, x * NZ + z), behind, here).start()

            @pl.when(x == y)
            def _():
                box[c, y] = src[...]

        def post(self, src, to, behind, s):
            return remote(src, self.box.at[c, y], to, s, arrive.at[self.k, behind])

        def arrived(self):
            for behind in (1, 3, 2, 0):
                src = (y + behind) % NY
                land = self.box.at[c, src]

                def wait():
                    remote(land, land, to_core, 0, arrive.at[self.k, behind]).wait_recv()

                if behind:
                    wait()
                else:
                    pl.when(x != y)(wait)
                push(land, land, to_core, self.s, self.r)

        def keep(self, cc):
            for src in range(NY):
                hi, lo = split(self.box[cc, src])
                self.kept[cc, 0, src] = hi
                self.kept[cc, 1, src] = lo

        def finish(self):
            self.keep(c)
            got(self.box.at[0], self.r)
            self.keep(oc)

    def partial(kept, weight):
        rows = kept.shape[-2]
        total = jnp.zeros((NY * rows, MD), F32)
        for cc in range(2):
            hi = kept[cc, 0].reshape(NY * rows, MD)
            lo = kept[cc, 1].reshape(NY * rows, MD)
            total = total + dot3(hi, lo, weight(cc).reshape(MD, MD))
        return total.reshape(NY, rows, MD)

    def panel(j, k):
        return lambda cc: pt[j, k, 4 * cc:4 * cc + 4]

    class YSum:
        def __init__(self, mine, theirs):
            self.mine, self.theirs, self.r = mine, theirs, fresh("recv")
            s = group(theirs)
            for n, (yy, to) in enumerate(((y_op, to_y_op), (y_up, to_y_up), (y_dn, to_y_dn))):
                push(mine.at[yy], theirs.at[n], to, s, self.r)

        def total(self):
            got(self.theirs, self.r)
            return (self.mine[y] + self.theirs[0]) + (self.theirs[1] + self.theirs[2])

    class YRelay:
        def __init__(self, j):
            self.j, self.s = j, group(rs.at[j])
            self.r = [fresh("recv") for _ in range(3)]
            for h, to in enumerate((to_y_up, to_y_dn)):
                push(part.at[j, y_op, halves[h]], rs.at[j, 2, halves[h]], to, self.s, self.r[h])
            self.pass_on(0, y_up, 1, to_y_up)
            self.pass_on(1, y_dn, 0, to_y_dn)

        def pass_on(self, way, yy, h, to):
            push(part.at[self.j, yy, halves[h]], rs.at[self.j, way, halves[h]], to, self.s, self.r[2])

        def forward(self):
            j = self.j
            for h, yy, to in ((0, y_up, to_y_up), (1, y_dn, to_y_dn)):
                got(rs.at[j, 2, halves[h]], self.r[h])
                part[j, yy, halves[h]] = part[j, yy, halves[h]] + rs[j, 2, halves[h]]
                self.pass_on(h, yy, h, to)

        def store(self):
            j = self.j
            got(rs.at[j, pl.ds(0, 2)], self.r[2])
            rows = pl.ds(j * MD, MD)
            trail[rows] = rhs_v[rows] - (part[j, y] + (rs[j, 0] + rs[j, 1])).T

    local = []

    def bring(src, dst):
        copy = pltpu.make_async_copy(src, dst, loc.at[len(local)])
        local.append(copy)
        copy.start()

    bring(top_h, top_v)
    bring(inv_h.at[0], az.at[0, z])
    bring(cpl_h, xc)
    bring(inv_h.at[1], az.at[2, z])
    for j in range(CHUNKS):
        bring(pan_h.at[:, :, pl.ds(j * MD, MD)], pt.at[j, :, z])
    bring(rhs_h, rhs_v)

    barrier = pltpu.get_barrier_semaphore()
    peers = [(((x + dx) % NX) * 2 + c, ((y + dy) % NY) * NZ + z) for dx in range(NX) for dy in range(NY) if dx or dy]
    peers += [(row, y * NZ + at_z(d)) for d in range(1, NZ)] + [to_core]
    for peer in peers:
        pl.semaphore_signal(barrier, inc=1, device_id=peer, device_id_type=MESH)
    local[0].wait()
    xs[0] = top_v[0].T
    xs[2] = top_v[1].T
    for copy in local[1:4]:
        copy.wait()
    pl.semaphore_wait(barrier, len(peers))

    views = lambda i: (lambda p: az.at[i, p], lambda p, h: az.at[i, p, pl.ds(h * KH, KH)],
                       lambda n: az.at[i, pl.ds(0, n)])
    rings = [ZRing(lambda p, j=j: pt.at[j, :, p], lambda p, h, j=j: pt.at[j, :, p, pl.ds(h * KH, KH)],
                   lambda n, j=j: pt.at[j, :, pl.ds(0, n)]) for j in range(CHUNKS)]
    factor = lambda i: lambda cc: az[i, 4 * cc:4 * cc + 4]
    kept = lambda k: sh.at[k]
    spread = lambda k: Spread(k, xs.at[k], sb.at[k], sh.at[k])

    spread0 = spread(0)
    ring_a = ZRing(*views(2))
    ring_a.start()
    pair0 = ZPair(*views(0))
    spread_c = Spread(4, xc, cb, ch)
    spread2 = spread(2)
    pair0.forward()
    ring_a.advance()
    for copy in local[4:]:
        copy.wait()
    rings[0].start()
    spread0.arrived()
    spread_c.arrived()
    spread0.finish()
    ring_a.advance()
    rings[1].start()
    pair0.finish()
    part[4] = partial(kept(0), factor(0))
    sum_f = YSum(part.at[4], rs.at[4])
    spread_c.finish()
    spread2.arrived()
    ring_a.advance()
    spread2.finish()
    ring_a.advance()
    wp[...] = partial(ch, factor(2))
    sum_w = YSum(wp, wr)
    rings[0].advance()
    first = sum_f.total()
    xs[1] = first
    spread1 = spread(1)
    solved[0] = first.T
    part[5] = partial(kept(2), factor(2))
    az[1, z] = sum_w.total()
    pair_w = ZPair(*views(1))
    rings[1].advance()
    pair_w.forward()
    rings[2].start()
    rings[3].start()
    rings[0].advance()
    spread1.arrived()
    spread1.finish()
    rings[1].advance()
    pair_w.finish()
    part[5] = part[5] - partial(kept(1), factor(1))
    sum_s = YSum(part.at[5], rs.at[5])
    rings[2].advance()
    rings[3].advance()
    second = sum_s.total()
    xs[3] = second
    spread3 = spread(3)
    solved[1] = second.T
    rings[0].advance()
    rings[1].advance()
    rings[2].advance()
    rings[3].advance()
    rings[0].advance()
    part[0] = partial(kept(1), panel(0, 0))
    spread3.arrived()
    spread3.finish()
    sums = []
    part[0] = part[0] + partial(kept(3), panel(0, 1))
    sums.append(YRelay(0))
    rings[1].advance()
    part[1] = partial(kept(1), panel(1, 0)) + partial(kept(3), panel(1, 1))
    sums.append(YRelay(1))
    rings[2].advance()
    rings[3].advance()
    sums[0].forward()
    rings[2].advance()
    part[2] = partial(kept(1), panel(2, 0)) + partial(kept(3), panel(2, 1))
    sums.append(YRelay(2))
    sums[1].forward()
    rings[3].advance()
    part[3] = partial(kept(1), panel(3, 0)) + partial(kept(3), panel(3, 1))
    sums.append(YRelay(3))
    sums[2].forward()
    sums[3].forward()
    for s in sums:
        s.store()
    for ref, i, when in drains:
        wait = remote(ref, ref, to_core, i, recv.at[0]).wait_send
        if when is None:
            wait()
        else:
            pl.when(when)(wait)
    assert (used["send"], used["recv"], len(local)) == (N_SEND, N_RECV, N_LOCAL), used


def body(inv_diag, coupling, top_rhs, panel, rhs):
    hbm = pl.BlockSpec(memory_space=pltpu.HBM)
    vmem = pl.BlockSpec(memory_space=pltpu.VMEM)
    solved, trailing = pl.pallas_call(
        kernel,
        out_shape=(jax.ShapeDtypeStruct((2, MD, TD), F32), jax.ShapeDtypeStruct((CHUNKS * MD, TD), F32)),
        in_specs=[hbm] * 5,
        out_specs=(vmem, vmem),
        scratch_shapes=[
            pltpu.VMEM((3, NZ, KD, MD), F32),
            pltpu.VMEM((CHUNKS, 2, NZ, KD, MD), F32),
            pltpu.VMEM((4, TD, MD), F32),
            pltpu.VMEM((4, 2, NY, TD, MD), F32),
            pltpu.VMEM((4, 2, 2, NY, TD, MD), BF16),
            pltpu.VMEM((2, NY, KD, MD), F32),
            pltpu.VMEM((2, 2, NY, KD, MD), BF16),
            pltpu.VMEM((KD, MD), F32),
            pltpu.VMEM((CHUNKS + 2, NY, TD, MD), F32),
            pltpu.VMEM((CHUNKS + 2, NY - 1, TD, MD), F32),
            pltpu.VMEM((NY, KD, MD), F32),
            pltpu.VMEM((NY - 1, KD, MD), F32),
            pltpu.VMEM((2, MD, TD), F32),
            pltpu.VMEM((CHUNKS * MD, TD), F32),
            pltpu.SemaphoreType.DMA((N_SEND,)),
            pltpu.SemaphoreType.DMA((N_RECV,)),
            pltpu.SemaphoreType.DMA((5, NY)),
            pltpu.SemaphoreType.DMA((N_LOCAL,)),
        ],
        compiler_params=pltpu.CompilerParams(
            collective_id=0, has_side_effects=True, vmem_limit_bytes=62 * 1024 * 1024),
    )(jnp.swapaxes(inv_diag, 1, 2), coupling.T, top_rhs, jnp.swapaxes(panel, 1, 2), rhs)
    return solved, trailing


def solution(mesh):
    in_specs = (
        P(None, "row", "col"),
        P("row", "col"),
        P(None, "row", "col"),
        P(None, "row", "col"),
        P("row", "col"),
    )
    out_specs = (P(None, "row", "col"), P("row", "col"))
    return jax.shard_map(body, mesh=mesh, in_specs=in_specs, out_specs=out_specs, check_vma=False)
```

```python
import jax
import jax.numpy as jnp
from jax import lax
from jax.experimental import pallas as pl
from jax.experimental.pallas import tpu as pltpu
from jax.sharding import PartitionSpec as P

MESH = pl.DeviceIdType.MESH
F32 = jnp.float32
BF16 = jnp.bfloat16
NX, NY, NZ = 4, 4, 8
KD, MD, TD = 64, 256, 128
KH = KD // 2
CHUNKS = 4
N_SEND, N_RECV, N_LOCAL = 29, 46, 9


def split(v):
    hi = v.astype(BF16)
    lo = (v - hi.astype(F32)).astype(BF16)
    return hi, lo


def dot(a, b):
    return jnp.dot(a, b, preferred_element_type=F32)


def dot3(hi, lo, w):
    wh, wl = split(w)
    return dot(hi, wh) + (dot(lo, wh) + dot(hi, wl))


def kernel(inv_h, cpl_h, top_h, pan_h, rhs_h, solved, trail,
           az, pt, xs, sb, sh, cb, ch, xc, part, rs, wp, wr, top_v, rhs_v, send, recv, arrive, loc):
    row, col = lax.axis_index("row"), lax.axis_index("col")
    x, c = row // 2, row % 2
    y, z = col // NZ, col % NZ
    oc = 1 - c
    x_up, x_dn, x_op = (x + 1) % NX, (x + NX - 1) % NX, (x + 2) % NX
    y_up, y_dn, y_op = (y + 1) % NY, (y + NY - 1) % NY, (y + 2) % NY
    to_x_up, to_x_dn = (x_up * 2 + c, col), (x_dn * 2 + c, col)
    to_y_up, to_y_dn, to_y_op = (row, y_up * NZ + z), (row, y_dn * NZ + z), (row, y_op * NZ + z)
    to_z_up, to_z_dn = (row, y * NZ + (z + 1) % NZ), (row, y * NZ + (z + NZ - 1) % NZ)
    to_x_op = (x_op * 2 + c, col)
    to_core = (x * 2 + oc, col)

    halves = (pl.ds(0, TD // 2), pl.ds(TD // 2, TD // 2))

    def at_z(d):
        return (z + NZ + d) % NZ

    used = {"send": 0, "recv": 0}
    drains = []

    def fresh(kind):
        used[kind] += 1
        return used[kind] - 1

    def group(ref, when=None):
        s = fresh("send")
        drains.append((ref, s, when))
        return s

    def remote(src, dst, to, s, sem):
        return pltpu.make_async_remote_copy(
            src_ref=src, dst_ref=dst, send_sem=send.at[s], recv_sem=sem, device_id=to, device_id_type=MESH)

    def push(src, dst, to, s, r):
        remote(src, dst, to, s, recv.at[r]).start()

    def move(view, at, to, s, r):
        push(view(at), view(at), to, s, r)

    def got(ref, r):
        remote(ref, ref, to_core, 0, recv.at[r]).wait_recv()

    class ZRing:
        def __init__(self, full, half, run):
            self.full, self.half, self.run, self.hop, self.s = full, half, run, 0, group(run(7))

        def start(self):
            s = self.hop
            up, dn = (z + NZ - s) % NZ, (z + s) % NZ
            self.r = fresh("recv")
            for at, to, h in ((up, to_z_up, 0), (dn, to_z_dn, 1)):
                move(self.full if s < 3 else lambda p: self.half(p, h), at, to, self.s, self.r)

        def advance(self):
            got(self.run(2 if self.hop < 3 else 1), self.r)
            self.hop += 1
            if self.hop < 4:
                self.start()

    class ZPair:
        def __init__(self, full, half, run):
            self.full, self.half, self.run, self.s = full, half, run, group(run(7))
            self.r = [fresh("recv") for _ in range(3)]
            for d in (2, -2, 1, -1):
                move(full, z, (row, y * NZ + at_z(d)), self.s, self.r[abs(d) - 1])

        def forward(self):
            far_up, far_dn = (row, y * NZ + at_z(2)), (row, y * NZ + at_z(-2))
            got(self.run(2), self.r[0])
            move(self.full, at_z(-1), far_up, self.s, self.r[2])
            move(self.full, at_z(1), far_dn, self.s, self.r[2])
            got(self.run(2), self.r[1])
            move(lambda p: self.half(p, 0), at_z(-2), far_up, self.s, self.r[2])
            move(lambda p: self.half(p, 1), at_z(2), far_dn, self.s, self.r[2])

        def finish(self):
            got(self.run(3), self.r[2])

    class Spread:
        def __init__(self, k, src, box, kept):
            self.k, self.box, self.kept = k, box, kept
            self.s, self.r = group(box.at[0]), fresh("recv")
            behind = (y + NY - x) % NY
            here = group(src, x != y)
            there = group(box.at[0, pl.ds(0, 3)])
            for xx in (x_op, x_up, x_dn):
                self.post(src, (xx * 2 + c, x * NZ + z), behind, there).start()

            @pl.when(x != y)
            def _():
                self.post(src, (row, x * NZ + z), behind, here).start()

            @pl.when(x == y)
            def _():
                box[c, y] = src[...]

        def post(self, src, to, behind, s):
            return remote(src, self.box.at[c, y], to, s, arrive.at[self.k, behind])

        def arrived(self):
            for behind in (1, 3, 2, 0):
                src = (y + behind) % NY
                land = self.box.at[c, src]

                def wait():
                    remote(land, land, to_core, 0, arrive.at[self.k, behind]).wait_recv()

                if behind:
                    wait()
                else:
                    pl.when(x != y)(wait)
                push(land, land, to_core, self.s, self.r)

        def keep(self, cc):
            for src in range(NY):
                hi, lo = split(self.box[cc, src])
                self.kept[cc, 0, src] = hi
                self.kept[cc, 1, src] = lo

        def finish(self):
            self.keep(c)
            got(self.box.at[0], self.r)
            self.keep(oc)

    def partial(kept, weight):
        rows = kept.shape[-2]
        total = jnp.zeros((NY * rows, MD), F32)
        for cc in range(2):
            hi = kept[cc, 0].reshape(NY * rows, MD)
            lo = kept[cc, 1].reshape(NY * rows, MD)
            total = total + dot3(hi, lo, weight(cc).reshape(MD, MD))
        return total.reshape(NY, rows, MD)

    def panel(j, k):
        return lambda cc: pt[j, k, 4 * cc:4 * cc + 4]

    class YSum:
        def __init__(self, mine, theirs):
            self.mine, self.theirs, self.r = mine, theirs, fresh("recv")
            s = group(theirs)
            for n, (yy, to) in enumerate(((y_op, to_y_op), (y_up, to_y_up), (y_dn, to_y_dn))):
                push(mine.at[yy], theirs.at[n], to, s, self.r)

        def total(self):
            got(self.theirs, self.r)
            return (self.mine[y] + self.theirs[0]) + (self.theirs[1] + self.theirs[2])

    class YRelay:
        def __init__(self, j):
            self.j, self.s = j, group(rs.at[j])
            self.r = [fresh("recv") for _ in range(3)]
            for h, to in enumerate((to_y_up, to_y_dn)):
                push(part.at[j, y_op, halves[h]], rs.at[j, 2, halves[h]], to, self.s, self.r[h])
            self.pass_on(0, y_up, 1, to_y_up)
            self.pass_on(1, y_dn, 0, to_y_dn)

        def pass_on(self, way, yy, h, to):
            push(part.at[self.j, yy, halves[h]], rs.at[self.j, way, halves[h]], to, self.s, self.r[2])

        def forward(self):
            j = self.j
            for h, yy, to in ((0, y_up, to_y_up), (1, y_dn, to_y_dn)):
                got(rs.at[j, 2, halves[h]], self.r[h])
                part[j, yy, halves[h]] = part[j, yy, halves[h]] + rs[j, 2, halves[h]]
                self.pass_on(h, yy, h, to)

        def store(self):
            j = self.j
            got(rs.at[j, pl.ds(0, 2)], self.r[2])
            rows = pl.ds(j * MD, MD)
            trail[rows] = rhs_v[rows] - (part[j, y] + (rs[j, 0] + rs[j, 1])).T

    local = []

    def bring(src, dst):
        copy = pltpu.make_async_copy(src, dst, loc.at[len(local)])
        local.append(copy)
        copy.start()

    bring(top_h, top_v)
    bring(inv_h.at[0], az.at[0, z])
    bring(cpl_h, xc)
    bring(inv_h.at[1], az.at[2, z])
    for j in range(CHUNKS):
        bring(pan_h.at[:, :, pl.ds(j * MD, MD)], pt.at[j, :, z])
    bring(rhs_h, rhs_v)

    barrier = pltpu.get_barrier_semaphore()
    peers = [(((x + dx) % NX) * 2 + c, ((y + dy) % NY) * NZ + z) for dx in range(NX) for dy in range(NY) if dx or dy]
    peers += [(row, y * NZ + at_z(d)) for d in range(1, NZ)] + [to_core]
    for peer in peers:
        pl.semaphore_signal(barrier, inc=1, device_id=peer, device_id_type=MESH)
    local[0].wait()
    xs[0] = top_v[0].T
    xs[2] = top_v[1].T
    for copy in local[1:4]:
        copy.wait()
    pl.semaphore_wait(barrier, len(peers))

    views = lambda i: (lambda p: az.at[i, p], lambda p, h: az.at[i, p, pl.ds(h * KH, KH)],
                       lambda n: az.at[i, pl.ds(0, n)])
    rings = [ZRing(lambda p, j=j: pt.at[j, :, p], lambda p, h, j=j: pt.at[j, :, p, pl.ds(h * KH, KH)],
                   lambda n, j=j: pt.at[j, :, pl.ds(0, n)]) for j in range(CHUNKS)]
    factor = lambda i: lambda cc: az[i, 4 * cc:4 * cc + 4]
    kept = lambda k: sh.at[k]
    spread = lambda k: Spread(k, xs.at[k], sb.at[k], sh.at[k])

    spread_c = Spread(4, xc, cb, ch)
    pair_a = ZPair(*views(2))
    ring_0 = ZRing(*views(0))
    ring_0.start()
    spread0 = spread(0)
    spread2 = spread(2)
    pair_a.forward()
    ring_0.advance()
    for copy in local[4:]:
        copy.wait()
    rings[0].start()
    spread_c.arrived()
    spread0.arrived()
    spread_c.finish()
    ring_0.advance()
    rings[1].start()
    pair_a.finish()
    wp[...] = partial(ch, factor(2))
    sum_w = YSum(wp, wr)
    spread0.finish()
    spread2.arrived()
    ring_0.advance()
    spread2.finish()
    rings[2].start()
    ring_0.advance()
    part[4] = partial(kept(0), factor(0))
    sum_f = YSum(part.at[4], rs.at[4])
    az[1, z] = sum_w.total()
    pair_w = ZPair(*views(1))
    rings[3].start()
    part[5] = partial(kept(2), factor(2))
    first = sum_f.total()
    xs[1] = first
    spread1 = spread(1)
    solved[0] = first.T
    pair_w.forward()
    rings[0].advance()
    rings[1].advance()
    rings[2].advance()
    spread1.arrived()
    pair_w.finish()
    spread1.finish()
    part[5] = part[5] - partial(kept(1), factor(1))
    sum_s = YSum(part.at[5], rs.at[5])
    rings[0].advance()
    rings[3].advance()
    rings[1].advance()
    second = sum_s.total()
    xs[3] = second
    spread3 = spread(3)
    solved[1] = second.T
    rings[0].advance()
    rings[2].advance()
    rings[1].advance()
    rings[3].advance()
    rings[0].advance()
    part[0] = partial(kept(1), panel(0, 0))
    spread3.arrived()
    spread3.finish()
    sums = []
    part[0] = part[0] + partial(kept(3), panel(0, 1))
    sums.append(YRelay(0))
    rings[2].advance()
    rings[1].advance()
    part[1] = partial(kept(1), panel(1, 0)) + partial(kept(3), panel(1, 1))
    sums.append(YRelay(1))
    rings[3].advance()
    rings[2].advance()
    part[2] = partial(kept(1), panel(2, 0)) + partial(kept(3), panel(2, 1))
    sums.append(YRelay(2))
    sums[0].forward()
    sums[1].forward()
    rings[3].advance()
    part[3] = partial(kept(1), panel(3, 0)) + partial(kept(3), panel(3, 1))
    sums.append(YRelay(3))
    sums[2].forward()
    sums[3].forward()
    for s in sums:
        s.store()
    for ref, i, when in drains:
        wait = remote(ref, ref, to_core, i, recv.at[0]).wait_send
        if when is None:
            wait()
        else:
            pl.when(when)(wait)
    assert (used["send"], used["recv"], len(local)) == (N_SEND, N_RECV, N_LOCAL), used


def body(inv_diag, coupling, top_rhs, panel, rhs):
    hbm = pl.BlockSpec(memory_space=pltpu.HBM)
    vmem = pl.BlockSpec(memory_space=pltpu.VMEM)
    operands = (jnp.swapaxes(inv_diag, 1, 2), coupling.T, top_rhs, jnp.swapaxes(panel, 1, 2), rhs)
    solved, trailing = pl.pallas_call(
        kernel,
        out_shape=(jax.ShapeDtypeStruct((2, MD, TD), F32), jax.ShapeDtypeStruct((CHUNKS * MD, TD), F32)),
        in_specs=[hbm] * 5,
        out_specs=(vmem, vmem),
        scratch_shapes=[
            pltpu.VMEM((3, NZ, KD, MD), F32),
            pltpu.VMEM((CHUNKS, 2, NZ, KD, MD), F32),
            pltpu.VMEM((4, TD, MD), F32),
            pltpu.VMEM((4, 2, NY, TD, MD), F32),
            pltpu.VMEM((4, 2, 2, NY, TD, MD), BF16),
            pltpu.VMEM((2, NY, KD, MD), F32),
            pltpu.VMEM((2, 2, NY, KD, MD), BF16),
            pltpu.VMEM((KD, MD), F32),
            pltpu.VMEM((CHUNKS + 2, NY, TD, MD), F32),
            pltpu.VMEM((CHUNKS + 2, NY - 1, TD, MD), F32),
            pltpu.VMEM((NY, KD, MD), F32),
            pltpu.VMEM((NY - 1, KD, MD), F32),
            pltpu.VMEM((2, MD, TD), F32),
            pltpu.VMEM((CHUNKS * MD, TD), F32),
            pltpu.SemaphoreType.DMA((N_SEND,)),
            pltpu.SemaphoreType.DMA((N_RECV,)),
            pltpu.SemaphoreType.DMA((5, NY)),
            pltpu.SemaphoreType.DMA((N_LOCAL,)),
        ],
        compiler_params=pltpu.CompilerParams(
            collective_id=0, has_side_effects=True, vmem_limit_bytes=32 * 1024 * 1024),
    )(*(pltpu.with_memory_space_constraint(v, pltpu.HBM) for v in operands))
    return solved, trailing


def solution(mesh):
    in_specs = (
        P(None, "row", "col"),
        P("row", "col"),
        P(None, "row", "col"),
        P(None, "row", "col"),
        P("row", "col"),
    )
    out_specs = (P(None, "row", "col"), P("row", "col"))
    return jax.shard_map(body, mesh=mesh, in_specs=in_specs, out_specs=out_specs, check_vma=False)
```

```python
import jax
import jax.numpy as jnp
from jax import lax
from jax.experimental import pallas as pl
from jax.experimental.pallas import tpu as pltpu
from jax.sharding import PartitionSpec as P

MESH = pl.DeviceIdType.MESH
F32 = jnp.float32
BF16 = jnp.bfloat16
NX, NY, NZ = 4, 4, 8
KD, MD, TD = 64, 256, 128
KH = KD // 2
CHUNKS = 4
N_SEND, N_RECV, N_LOCAL = 37, 52, 9


def split(v):
    hi = v.astype(BF16)
    lo = (v - hi.astype(F32)).astype(BF16)
    return hi, lo


def dot(a, b):
    return jnp.dot(a, b, preferred_element_type=F32)


def dot3(hi, lo, w):
    wh, wl = split(w)
    return dot(hi, wh) + (dot(lo, wh) + dot(hi, wl))


def kernel(inv_h, cpl_h, top_h, pan_h, rhs_h, solved, trail,
           az, pt, xs, sb, sh, sbh, shh, cb, ch, xc, part, rs, wp, wr, top_v, rhs_v, send, recv, arrive, loc):
    row, col = lax.axis_index("row"), lax.axis_index("col")
    x, c = row // 2, row % 2
    y, z = col // NZ, col % NZ
    oc = 1 - c
    x_up, x_dn, x_op = (x + 1) % NX, (x + NX - 1) % NX, (x + 2) % NX
    y_up, y_dn, y_op = (y + 1) % NY, (y + NY - 1) % NY, (y + 2) % NY
    to_x_up, to_x_dn = (x_up * 2 + c, col), (x_dn * 2 + c, col)
    to_y_up, to_y_dn, to_y_op = (row, y_up * NZ + z), (row, y_dn * NZ + z), (row, y_op * NZ + z)
    to_z_up, to_z_dn = (row, y * NZ + (z + 1) % NZ), (row, y * NZ + (z + NZ - 1) % NZ)
    to_x_op = (x_op * 2 + c, col)
    to_core = (x * 2 + oc, col)

    halves = (pl.ds(0, TD // 2), pl.ds(TD // 2, TD // 2))

    def at_z(d):
        return (z + NZ + d) % NZ

    used = {"send": 0, "recv": 0}
    drains = []

    def fresh(kind):
        used[kind] += 1
        return used[kind] - 1

    def group(ref, when=None):
        s = fresh("send")
        drains.append((ref, s, when))
        return s

    def remote(src, dst, to, s, sem):
        return pltpu.make_async_remote_copy(
            src_ref=src, dst_ref=dst, send_sem=send.at[s], recv_sem=sem, device_id=to, device_id_type=MESH)

    def push(src, dst, to, s, r):
        remote(src, dst, to, s, recv.at[r]).start()

    def move(view, at, to, s, r):
        push(view(at), view(at), to, s, r)

    def got(ref, r):
        remote(ref, ref, to_core, 0, recv.at[r]).wait_recv()

    class ZRing:
        def __init__(self, full, half, run):
            self.full, self.half, self.run, self.hop, self.s = full, half, run, 0, group(run(7))

        def start(self):
            s = self.hop
            up, dn = (z + NZ - s) % NZ, (z + s) % NZ
            self.r = fresh("recv")
            for at, to, h in ((up, to_z_up, 0), (dn, to_z_dn, 1)):
                move(self.full if s < 3 else lambda p: self.half(p, h), at, to, self.s, self.r)

        def advance(self):
            got(self.run(2 if self.hop < 3 else 1), self.r)
            self.hop += 1
            if self.hop < 4:
                self.start()

    class ZPair:
        def __init__(self, full, half, run):
            self.full, self.half, self.run, self.s = full, half, run, group(run(7))
            self.r = [fresh("recv") for _ in range(3)]
            for d in (2, -2, 1, -1):
                move(full, z, (row, y * NZ + at_z(d)), self.s, self.r[abs(d) - 1])

        def forward(self):
            far_up, far_dn = (row, y * NZ + at_z(2)), (row, y * NZ + at_z(-2))
            got(self.run(2), self.r[0])
            move(self.full, at_z(-1), far_up, self.s, self.r[2])
            move(self.full, at_z(1), far_dn, self.s, self.r[2])
            got(self.run(2), self.r[1])
            move(lambda p: self.half(p, 0), at_z(-2), far_up, self.s, self.r[2])
            move(lambda p: self.half(p, 1), at_z(2), far_dn, self.s, self.r[2])

        def finish(self):
            got(self.run(3), self.r[2])

    class Spread:
        def __init__(self, k, src, box, kept):
            self.k, self.box, self.kept = k, box, kept
            self.s, self.r = group(box.at[0]), fresh("recv")
            behind = (y + NY - x) % NY
            here = group(src, x != y)
            there = group(box.at[0, pl.ds(0, 3)])
            for xx in (x_op, x_up, x_dn):
                self.post(src, (xx * 2 + c, x * NZ + z), behind, there).start()

            @pl.when(x != y)
            def _():
                self.post(src, (row, x * NZ + z), behind, here).start()

            @pl.when(x == y)
            def _():
                box[c, y] = src[...]

        def post(self, src, to, behind, s):
            return remote(src, self.box.at[c, y], to, s, arrive.at[self.k, behind])

        def arrived(self):
            for behind in (1, 3, 2, 0):
                src = (y + behind) % NY
                land = self.box.at[c, src]

                def wait():
                    remote(land, land, to_core, 0, arrive.at[self.k, behind]).wait_recv()

                if behind:
                    wait()
                else:
                    pl.when(x != y)(wait)
                push(land, land, to_core, self.s, self.r)

        def keep(self, cc):
            for src in range(NY):
                hi, lo = split(self.box[cc, src])
                self.kept[cc, 0, src] = hi
                self.kept[cc, 1, src] = lo

        def finish(self):
            self.keep(c)
            got(self.box.at[0], self.r)
            self.keep(oc)

    def partial(kept, weight):
        rows = kept.shape[-2]
        total = jnp.zeros((NY * rows, MD), F32)
        for cc in range(2):
            hi = kept[cc, 0].reshape(NY * rows, MD)
            lo = kept[cc, 1].reshape(NY * rows, MD)
            total = total + dot3(hi, lo, weight(cc).reshape(MD, MD))
        return total.reshape(NY, rows, MD)

    def panel(j, k):
        return lambda cc: pt[j, k, 4 * cc:4 * cc + 4]

    class YSum:
        def __init__(self, mine, theirs, span=slice(None)):
            self.mine, self.theirs, self.span, self.r = mine, theirs, span, fresh("recv")
            s = group(theirs.at[:, span])
            for n, (yy, to) in enumerate(((y_op, to_y_op), (y_up, to_y_up), (y_dn, to_y_dn))):
                push(mine.at[yy, span], theirs.at[n, span], to, s, self.r)

        def total(self):
            mine, theirs, span = self.mine, self.theirs, self.span
            got(theirs.at[:, span], self.r)
            return (mine[y, span] + theirs[0, span]) + (theirs[1, span] + theirs[2, span])

    class YRelay:
        def __init__(self, j, h):
            self.j, self.h, self.s = j, h, group(rs.at[j, :, halves[h]])
            self.r = [fresh("recv") for _ in range(2)]
            self.via, self.to = ((y_up, to_y_up), (y_dn, to_y_dn))[h]
            other, to_other = ((y_dn, to_y_dn), (y_up, to_y_up))[h]
            push(part.at[j, y_op, halves[h]], rs.at[j, 2, halves[h]], self.to, self.s, self.r[0])
            self.pass_on(1 - h, other, to_other)

        def pass_on(self, way, yy, to):
            half = halves[self.h]
            push(part.at[self.j, yy, half], rs.at[self.j, way, half], to, self.s, self.r[1])

        def forward(self):
            j, half = self.j, halves[self.h]
            got(rs.at[j, 2, half], self.r[0])
            part[j, self.via, half] = part[j, self.via, half] + rs[j, 2, half]
            self.pass_on(self.h, self.via, self.to)

        def finish(self):
            got(rs.at[self.j, pl.ds(0, 2), halves[self.h]], self.r[1])

    def store(j):
        rows = pl.ds(j * MD, MD)
        trail[rows] = rhs_v[rows] - (part[j, y] + (rs[j, 0] + rs[j, 1])).T

    def first_part(j):
        part[j] = partial(kept(1), panel(j, 0))

    def second_part(j, h):
        part[j, :, halves[h]] = part[j, :, halves[h]] + partial(shh.at[h], panel(j, 1))
        return YRelay(j, h)

    local = []

    def bring(src, dst):
        copy = pltpu.make_async_copy(src, dst, loc.at[len(local)])
        local.append(copy)
        copy.start()

    bring(top_h, top_v)
    bring(inv_h.at[0], az.at[0, z])
    bring(cpl_h, xc)
    bring(inv_h.at[1], az.at[2, z])
    for j in range(CHUNKS):
        bring(pan_h.at[:, :, pl.ds(j * MD, MD)], pt.at[j, :, z])
    bring(rhs_h, rhs_v)

    barrier = pltpu.get_barrier_semaphore()
    peers = [(((x + dx) % NX) * 2 + c, ((y + dy) % NY) * NZ + z) for dx in range(NX) for dy in range(NY) if dx or dy]
    peers += [(row, y * NZ + at_z(d)) for d in range(1, NZ)] + [to_core]
    for peer in peers:
        pl.semaphore_signal(barrier, inc=1, device_id=peer, device_id_type=MESH)
    local[0].wait()
    xs[0] = top_v[0].T
    xs[2] = top_v[1].T
    for copy in local[1:4]:
        copy.wait()
    pl.semaphore_wait(barrier, len(peers))

    views = lambda i: (lambda p: az.at[i, p], lambda p, h: az.at[i, p, pl.ds(h * KH, KH)],
                       lambda n: az.at[i, pl.ds(0, n)])
    rings = [ZRing(lambda p, j=j: pt.at[j, :, p], lambda p, h, j=j: pt.at[j, :, p, pl.ds(h * KH, KH)],
                   lambda n, j=j: pt.at[j, :, pl.ds(0, n)]) for j in range(CHUNKS)]
    factor = lambda i: lambda cc: az[i, 4 * cc:4 * cc + 4]
    kept = lambda k: sh.at[k]
    spread = lambda k: Spread(k, xs.at[k], sb.at[k], sh.at[k])

    spread_c = Spread(4, xc, cb, ch)
    pair_a = ZPair(*views(2))
    ring_0 = ZRing(*views(0))
    ring_0.start()
    spread0 = spread(0)
    spread2 = spread(2)
    pair_a.forward()
    ring_0.advance()
    for copy in local[4:]:
        copy.wait()
    rings[0].start()
    spread_c.arrived()
    spread0.arrived()
    spread_c.finish()
    ring_0.advance()
    rings[1].start()
    pair_a.finish()
    wp[...] = partial(ch, factor(2))
    sum_w = YSum(wp, wr)
    spread0.finish()
    spread2.arrived()
    ring_0.advance()
    spread2.finish()
    az[1, z] = sum_w.total()
    pair_w = ZPair(*views(1))
    ring_0.advance()
    part[4] = partial(kept(0), factor(0))
    sum_f = YSum(part.at[4], rs.at[4])
    rings[0].advance()
    rings[2].start()
    part[5] = partial(kept(2), factor(2))
    first = sum_f.total()
    xs[1] = first
    spread1 = spread(1)
    solved[0] = first.T
    pair_w.forward()
    rings[0].advance()
    rings[1].advance()
    rings[3].start()
    spread1.arrived()
    pair_w.finish()
    spread1.finish()
    part[5] = part[5] - partial(kept(1), factor(1))
    sums_s = [YSum(part.at[5], rs.at[5], half) for half in halves]
    rings[0].advance()
    rings[1].advance()
    rings[2].advance()
    spreads3 = []
    for h in range(2):
        xs[3, halves[h]] = sums_s[h].total()
        spreads3.append(Spread((3, 5)[h], xs.at[3, halves[h]], sbh.at[h], shh.at[h]))
    solved[1] = xs[3].T
    rings[0].advance()
    rings[1].advance()
    rings[3].advance()
    first_part(0)
    rings[2].advance()
    spreads3[0].arrived()
    spreads3[1].arrived()
    spreads3[0].finish()
    relays = [second_part(0, 0)]
    rings[1].advance()
    rings[3].advance()
    spreads3[1].finish()
    relays.append(second_part(0, 1))
    rings[2].advance()
    first_part(1)
    relays.append(second_part(1, 0))
    relays.append(second_part(1, 1))
    relays[0].forward()
    rings[3].advance()
    relays[1].forward()
    rings[2].advance()
    first_part(2)
    relays[2].forward()
    relays.append(second_part(2, 0))
    relays.append(second_part(2, 1))
    relays[3].forward()
    rings[3].advance()
    first_part(3)
    relays.append(second_part(3, 0))
    relays.append(second_part(3, 1))
    for relay in relays[4:]:
        relay.forward()
    for relay in relays[:4]:
        relay.finish()
    store(0)
    store(1)
    for relay in relays[4:6]:
        relay.finish()
    store(2)
    for relay in relays[6:]:
        relay.finish()
    store(3)
    for ref, i, when in drains:
        wait = remote(ref, ref, to_core, i, recv.at[0]).wait_send
        if when is None:
            wait()
        else:
            pl.when(when)(wait)
    assert (used["send"], used["recv"], len(local)) == (N_SEND, N_RECV, N_LOCAL), used


def body(inv_diag, coupling, top_rhs, panel, rhs):
    hbm = pl.BlockSpec(memory_space=pltpu.HBM)
    vmem = pl.BlockSpec(memory_space=pltpu.VMEM)
    operands = (jnp.swapaxes(inv_diag, 1, 2), coupling.T, top_rhs, jnp.swapaxes(panel, 1, 2), rhs)
    solved, trailing = pl.pallas_call(
        kernel,
        out_shape=(jax.ShapeDtypeStruct((2, MD, TD), F32), jax.ShapeDtypeStruct((CHUNKS * MD, TD), F32)),
        in_specs=[hbm] * 5,
        out_specs=(vmem, vmem),
        scratch_shapes=[
            pltpu.VMEM((3, NZ, KD, MD), F32),
            pltpu.VMEM((CHUNKS, 2, NZ, KD, MD), F32),
            pltpu.VMEM((4, TD, MD), F32),
            pltpu.VMEM((3, 2, NY, TD, MD), F32),
            pltpu.VMEM((3, 2, 2, NY, TD, MD), BF16),
            pltpu.VMEM((2, 2, NY, TD // 2, MD), F32),
            pltpu.VMEM((2, 2, 2, NY, TD // 2, MD), BF16),
            pltpu.VMEM((2, NY, KD, MD), F32),
            pltpu.VMEM((2, 2, NY, KD, MD), BF16),
            pltpu.VMEM((KD, MD), F32),
            pltpu.VMEM((CHUNKS + 2, NY, TD, MD), F32),
            pltpu.VMEM((CHUNKS + 2, NY - 1, TD, MD), F32),
            pltpu.VMEM((NY, KD, MD), F32),
            pltpu.VMEM((NY - 1, KD, MD), F32),
            pltpu.VMEM((2, MD, TD), F32),
            pltpu.VMEM((CHUNKS * MD, TD), F32),
            pltpu.SemaphoreType.DMA((N_SEND,)),
            pltpu.SemaphoreType.DMA((N_RECV,)),
            pltpu.SemaphoreType.DMA((6, NY)),
            pltpu.SemaphoreType.DMA((N_LOCAL,)),
        ],
        compiler_params=pltpu.CompilerParams(
            collective_id=0, has_side_effects=True, vmem_limit_bytes=32 * 1024 * 1024),
    )(*(pltpu.with_memory_space_constraint(v, pltpu.HBM) for v in operands))
    return solved, trailing


def solution(mesh):
    in_specs = (
        P(None, "row", "col"),
        P("row", "col"),
        P(None, "row", "col"),
        P(None, "row", "col"),
        P("row", "col"),
    )
    out_specs = (P(None, "row", "col"), P("row", "col"))
    return jax.shard_map(body, mesh=mesh, in_specs=in_specs, out_specs=out_specs, check_vma=False)
```

```python
import jax
import jax.numpy as jnp
from jax import lax
from jax.experimental import pallas as pl
from jax.experimental.pallas import tpu as pltpu
from jax.sharding import PartitionSpec as P

MESH = pl.DeviceIdType.MESH
F32 = jnp.float32
BF16 = jnp.bfloat16
NX, NY, NZ = 4, 4, 8
KD, MD, TD = 64, 256, 128
KH = KD // 2
CHUNKS = 4
N_SEND, N_RECV, N_LOCAL = 37, 52, 9


def split(v):
    hi = v.astype(BF16)
    lo = (v - hi.astype(F32)).astype(BF16)
    return hi, lo


def dot(a, b):
    return jnp.dot(a, b, preferred_element_type=F32)


def dot3(hi, lo, w):
    wh, wl = split(w)
    return dot(hi, wh) + (dot(lo, wh) + dot(hi, wl))


def kernel(inv_h, cpl_h, top_h, pan_h, rhs_h, solved, trail,
           az, pt, xs, sb, sh, sbh, shh, cb, ch, xc, part, rs, wp, wr, top_v, rhs_v, send, recv, arrive, loc):
    row, col = lax.axis_index("row"), lax.axis_index("col")
    x, c = row // 2, row % 2
    y, z = col // NZ, col % NZ
    oc = 1 - c
    x_up, x_dn, x_op = (x + 1) % NX, (x + NX - 1) % NX, (x + 2) % NX
    y_up, y_dn, y_op = (y + 1) % NY, (y + NY - 1) % NY, (y + 2) % NY
    to_x_up, to_x_dn = (x_up * 2 + c, col), (x_dn * 2 + c, col)
    to_y_up, to_y_dn, to_y_op = (row, y_up * NZ + z), (row, y_dn * NZ + z), (row, y_op * NZ + z)
    to_z_up, to_z_dn = (row, y * NZ + (z + 1) % NZ), (row, y * NZ + (z + NZ - 1) % NZ)
    to_x_op = (x_op * 2 + c, col)
    to_core = (x * 2 + oc, col)

    halves = (pl.ds(0, TD // 2), pl.ds(TD // 2, TD // 2))

    def at_z(d):
        return (z + NZ + d) % NZ

    used = {"send": 0, "recv": 0}
    drains = []

    def fresh(kind):
        used[kind] += 1
        return used[kind] - 1

    def group(ref, when=None):
        s = fresh("send")
        drains.append((ref, s, when))
        return s

    def remote(src, dst, to, s, sem):
        return pltpu.make_async_remote_copy(
            src_ref=src, dst_ref=dst, send_sem=send.at[s], recv_sem=sem, device_id=to, device_id_type=MESH)

    def push(src, dst, to, s, r):
        remote(src, dst, to, s, recv.at[r]).start()

    def move(view, at, to, s, r):
        push(view(at), view(at), to, s, r)

    def got(ref, r):
        remote(ref, ref, to_core, 0, recv.at[r]).wait_recv()

    class ZRing:
        def __init__(self, full, half, run):
            self.full, self.half, self.run, self.hop, self.s = full, half, run, 0, group(run(7))

        def start(self):
            s = self.hop
            up, dn = (z + NZ - s) % NZ, (z + s) % NZ
            self.r = fresh("recv")
            for at, to, h in ((up, to_z_up, 0), (dn, to_z_dn, 1)):
                move(self.full if s < 3 else lambda p: self.half(p, h), at, to, self.s, self.r)

        def advance(self):
            got(self.run(2 if self.hop < 3 else 1), self.r)
            self.hop += 1
            if self.hop < 4:
                self.start()

    class ZPair:
        def __init__(self, full, half, run):
            self.full, self.half, self.run, self.s = full, half, run, group(run(7))
            self.r = [fresh("recv") for _ in range(3)]
            for d in (2, -2, 1, -1):
                move(full, z, (row, y * NZ + at_z(d)), self.s, self.r[abs(d) - 1])

        def forward(self):
            far_up, far_dn = (row, y * NZ + at_z(2)), (row, y * NZ + at_z(-2))
            got(self.run(2), self.r[0])
            move(self.full, at_z(-1), far_up, self.s, self.r[2])
            move(self.full, at_z(1), far_dn, self.s, self.r[2])
            got(self.run(2), self.r[1])
            move(lambda p: self.half(p, 0), at_z(-2), far_up, self.s, self.r[2])
            move(lambda p: self.half(p, 1), at_z(2), far_dn, self.s, self.r[2])

        def finish(self):
            got(self.run(3), self.r[2])

    class Spread:
        def __init__(self, k, src, box, kept):
            self.k, self.box, self.kept = k, box, kept
            self.s, self.r = group(box.at[0]), fresh("recv")
            behind = (y + NY - x) % NY
            here = group(src, x != y)
            there = group(box.at[0, pl.ds(0, 3)])
            for xx in (x_op, x_up, x_dn):
                self.post(src, (xx * 2 + c, x * NZ + z), behind, there).start()

            @pl.when(x != y)
            def _():
                self.post(src, (row, x * NZ + z), behind, here).start()

            @pl.when(x == y)
            def _():
                box[c, y] = src[...]

        def post(self, src, to, behind, s):
            return remote(src, self.box.at[c, y], to, s, arrive.at[self.k, behind])

        def arrived(self):
            for behind in (1, 3, 2, 0):
                src = (y + behind) % NY
                land = self.box.at[c, src]

                def wait():
                    remote(land, land, to_core, 0, arrive.at[self.k, behind]).wait_recv()

                if behind:
                    wait()
                else:
                    pl.when(x != y)(wait)
                push(land, land, to_core, self.s, self.r)

        def keep(self, cc):
            for src in range(NY):
                hi, lo = split(self.box[cc, src])
                self.kept[cc, 0, src] = hi
                self.kept[cc, 1, src] = lo

        def finish(self):
            self.keep(c)
            got(self.box.at[0], self.r)
            self.keep(oc)

    def partial(kept, weight):
        rows = kept.shape[-2]
        total = jnp.zeros((NY * rows, MD), F32)
        for cc in range(2):
            hi = kept[cc, 0].reshape(NY * rows, MD)
            lo = kept[cc, 1].reshape(NY * rows, MD)
            total = total + dot3(hi, lo, weight(cc).reshape(MD, MD))
        return total.reshape(NY, rows, MD)

    def panel(j, k):
        return lambda cc: pt[j, k, 4 * cc:4 * cc + 4]

    class YSum:
        def __init__(self, mine, theirs, span=slice(None)):
            self.mine, self.theirs, self.span, self.r = mine, theirs, span, fresh("recv")
            s = group(theirs.at[:, span])
            for n, (yy, to) in enumerate(((y_op, to_y_op), (y_up, to_y_up), (y_dn, to_y_dn))):
                push(mine.at[yy, span], theirs.at[n, span], to, s, self.r)

        def total(self):
            mine, theirs, span = self.mine, self.theirs, self.span
            got(theirs.at[:, span], self.r)
            return (mine[y, span] + theirs[0, span]) + (theirs[1, span] + theirs[2, span])

    class YRelay:
        def __init__(self, j, h):
            self.j, self.h, self.s = j, h, group(rs.at[j, :, halves[h]])
            self.r = [fresh("recv") for _ in range(2)]
            self.via, self.to = ((y_up, to_y_up), (y_dn, to_y_dn))[h]
            other, to_other = ((y_dn, to_y_dn), (y_up, to_y_up))[h]
            push(part.at[j, y_op, halves[h]], rs.at[j, 2, halves[h]], self.to, self.s, self.r[0])
            self.pass_on(1 - h, other, to_other)

        def pass_on(self, way, yy, to):
            half = halves[self.h]
            push(part.at[self.j, yy, half], rs.at[self.j, way, half], to, self.s, self.r[1])

        def forward(self):
            j, half = self.j, halves[self.h]
            got(rs.at[j, 2, half], self.r[0])
            part[j, self.via, half] = part[j, self.via, half] + rs[j, 2, half]
            self.pass_on(self.h, self.via, self.to)

        def finish(self):
            got(rs.at[self.j, pl.ds(0, 2), halves[self.h]], self.r[1])

    def store(j):
        rows = pl.ds(j * MD, MD)
        trail[rows] = rhs_v[rows] - (part[j, y] + (rs[j, 0] + rs[j, 1])).T

    def first_part(j):
        part[j] = partial(kept(1), panel(j, 0))

    def second_part(j, h):
        part[j, :, halves[h]] = part[j, :, halves[h]] + partial(shh.at[h], panel(j, 1))
        return YRelay(j, h)

    local = []

    def bring(src, dst):
        copy = pltpu.make_async_copy(src, dst, loc.at[len(local)])
        local.append(copy)
        copy.start()

    bring(top_h, top_v)
    bring(inv_h.at[0], az.at[0, z])
    bring(cpl_h, xc)
    bring(inv_h.at[1], az.at[2, z])
    for j in range(CHUNKS):
        bring(pan_h.at[:, :, pl.ds(j * MD, MD)], pt.at[j, :, z])
    bring(rhs_h, rhs_v)

    barrier = pltpu.get_barrier_semaphore()
    peers = [(((x + dx) % NX) * 2 + c, ((y + dy) % NY) * NZ + z) for dx in range(NX) for dy in range(NY) if dx or dy]
    peers += [(row, y * NZ + at_z(d)) for d in range(1, NZ)] + [to_core]
    for peer in peers:
        pl.semaphore_signal(barrier, inc=1, device_id=peer, device_id_type=MESH)
    local[0].wait()
    xs[0] = top_v[0].T
    xs[2] = top_v[1].T
    for copy in local[1:4]:
        copy.wait()
    pl.semaphore_wait(barrier, len(peers))

    views = lambda i: (lambda p: az.at[i, p], lambda p, h: az.at[i, p, pl.ds(h * KH, KH)],
                       lambda n: az.at[i, pl.ds(0, n)])
    rings = [ZRing(lambda p, j=j: pt.at[j, :, p], lambda p, h, j=j: pt.at[j, :, p, pl.ds(h * KH, KH)],
                   lambda n, j=j: pt.at[j, :, pl.ds(0, n)]) for j in range(CHUNKS)]
    factor = lambda i: lambda cc: az[i, 4 * cc:4 * cc + 4]
    kept = lambda k: sh.at[k]
    spread = lambda k: Spread(k, xs.at[k], sb.at[k], sh.at[k])

    spread_c = Spread(4, xc, cb, ch)
    pair_a = ZPair(*views(2))
    ring_0 = ZRing(*views(0))
    ring_0.start()
    spread0 = spread(0)
    spread2 = spread(2)
    pair_a.forward()
    ring_0.advance()
    for copy in local[4:]:
        copy.wait()
    rings[0].start()
    spread_c.arrived()
    spread0.arrived()
    spread_c.finish()
    ring_0.advance()
    rings[1].start()
    pair_a.finish()
    wp[...] = partial(ch, factor(2))
    sum_w = YSum(wp, wr)
    spread0.finish()
    spread2.arrived()
    ring_0.advance()
    spread2.finish()
    az[1, z] = sum_w.total()
    pair_w = ZPair(*views(1))
    ring_0.advance()
    part[4] = partial(kept(0), factor(0))
    sum_f = YSum(part.at[4], rs.at[4])
    rings[0].advance()
    rings[2].start()
    part[5] = partial(kept(2), factor(2))
    pair_w.forward()
    first = sum_f.total()
    xs[1] = first
    spread1 = spread(1)
    solved[0] = first.T
    rings[0].advance()
    rings[1].advance()
    rings[3].start()
    spread1.arrived()
    pair_w.finish()
    spread1.finish()
    part[5] = part[5] - partial(kept(1), factor(1))
    sums_s = [YSum(part.at[5], rs.at[5], half) for half in halves]
    rings[0].advance()
    rings[1].advance()
    rings[2].advance()
    rings[3].advance()
    spreads3 = []
    for h in range(2):
        xs[3, halves[h]] = sums_s[h].total()
        spreads3.append(Spread((3, 5)[h], xs.at[3, halves[h]], sbh.at[h], shh.at[h]))
    solved[1] = xs[3].T
    rings[0].advance()
    rings[1].advance()
    first_part(0)
    rings[2].advance()
    spreads3[0].arrived()
    spreads3[0].finish()
    relays = [second_part(0, 0)]
    spreads3[1].arrived()
    rings[3].advance()
    rings[1].advance()
    spreads3[1].finish()
    relays.append(second_part(0, 1))
    first_part(1)
    relays.append(second_part(1, 0))
    rings[2].advance()
    relays.append(second_part(1, 1))
    relays[0].forward()
    rings[3].advance()
    relays[1].forward()
    rings[2].advance()
    first_part(2)
    relays[2].forward()
    relays.append(second_part(2, 0))
    relays.append(second_part(2, 1))
    relays[3].forward()
    rings[3].advance()
    first_part(3)
    relays.append(second_part(3, 0))
    relays.append(second_part(3, 1))
    for relay in relays[4:]:
        relay.forward()
    for relay in relays[:4]:
        relay.finish()
    store(0)
    store(1)
    for relay in relays[4:6]:
        relay.finish()
    store(2)
    for relay in relays[6:]:
        relay.finish()
    store(3)
    for ref, i, when in drains:
        wait = remote(ref, ref, to_core, i, recv.at[0]).wait_send
        if when is None:
            wait()
        else:
            pl.when(when)(wait)
    assert (used["send"], used["recv"], len(local)) == (N_SEND, N_RECV, N_LOCAL), used


def body(inv_diag, coupling, top_rhs, panel, rhs):
    hbm = pl.BlockSpec(memory_space=pltpu.HBM)
    vmem = pl.BlockSpec(memory_space=pltpu.VMEM)
    operands = (jnp.swapaxes(inv_diag, 1, 2), coupling.T, top_rhs, jnp.swapaxes(panel, 1, 2), rhs)
    solved, trailing = pl.pallas_call(
        kernel,
        out_shape=(jax.ShapeDtypeStruct((2, MD, TD), F32), jax.ShapeDtypeStruct((CHUNKS * MD, TD), F32)),
        in_specs=[hbm] * 5,
        out_specs=(vmem, vmem),
        scratch_shapes=[
            pltpu.VMEM((3, NZ, KD, MD), F32),
            pltpu.VMEM((CHUNKS, 2, NZ, KD, MD), F32),
            pltpu.VMEM((4, TD, MD), F32),
            pltpu.VMEM((3, 2, NY, TD, MD), F32),
            pltpu.VMEM((3, 2, 2, NY, TD, MD), BF16),
            pltpu.VMEM((2, 2, NY, TD // 2, MD), F32),
            pltpu.VMEM((2, 2, 2, NY, TD // 2, MD), BF16),
            pltpu.VMEM((2, NY, KD, MD), F32),
            pltpu.VMEM((2, 2, NY, KD, MD), BF16),
            pltpu.VMEM((KD, MD), F32),
            pltpu.VMEM((CHUNKS + 2, NY, TD, MD), F32),
            pltpu.VMEM((CHUNKS + 2, NY - 1, TD, MD), F32),
            pltpu.VMEM((NY, KD, MD), F32),
            pltpu.VMEM((NY - 1, KD, MD), F32),
            pltpu.VMEM((2, MD, TD), F32),
            pltpu.VMEM((CHUNKS * MD, TD), F32),
            pltpu.SemaphoreType.DMA((N_SEND,)),
            pltpu.SemaphoreType.DMA((N_RECV,)),
            pltpu.SemaphoreType.DMA((6, NY)),
            pltpu.SemaphoreType.DMA((N_LOCAL,)),
        ],
        compiler_params=pltpu.CompilerParams(
            collective_id=0, has_side_effects=True, vmem_limit_bytes=32 * 1024 * 1024),
    )(*(pltpu.with_memory_space_constraint(v, pltpu.HBM) for v in operands))
    return solved, trailing


def solution(mesh):
    in_specs = (
        P(None, "row", "col"),
        P("row", "col"),
        P(None, "row", "col"),
        P(None, "row", "col"),
        P("row", "col"),
    )
    out_specs = (P(None, "row", "col"), P("row", "col"))
    return jax.shard_map(body, mesh=mesh, in_specs=in_specs, out_specs=out_specs, check_vma=False)
```

```python
import jax
import jax.numpy as jnp
from jax import lax
from jax.experimental import pallas as pl
from jax.experimental.pallas import tpu as pltpu
from jax.sharding import PartitionSpec as P

MESH = pl.DeviceIdType.MESH
F32 = jnp.float32
BF16 = jnp.bfloat16
NX, NY, NZ = 4, 4, 8
KD, MD, TD = 64, 256, 128
KH = KD // 2
CHUNKS = 4
N_SEND, N_RECV, N_LOCAL = 37, 52, 9


def split(v):
    hi = v.astype(BF16)
    lo = (v - hi.astype(F32)).astype(BF16)
    return hi, lo


def dot(a, b):
    return jnp.dot(a, b, preferred_element_type=F32)


def dot3(hi, lo, w):
    wh, wl = split(w)
    return dot(hi, wh) + (dot(lo, wh) + dot(hi, wl))


def kernel(inv_h, cpl_h, top_h, pan_h, rhs_h, solved, trail,
           az, pt, xs, sb, sh, sbh, shh, cb, ch, xc, part, rs, wp, wr, top_v, rhs_v, send, recv, arrive, loc):
    row, col = lax.axis_index("row"), lax.axis_index("col")
    x, c = row // 2, row % 2
    y, z = col // NZ, col % NZ
    oc = 1 - c
    x_up, x_dn, x_op = (x + 1) % NX, (x + NX - 1) % NX, (x + 2) % NX
    y_up, y_dn, y_op = (y + 1) % NY, (y + NY - 1) % NY, (y + 2) % NY
    to_x_up, to_x_dn = (x_up * 2 + c, col), (x_dn * 2 + c, col)
    to_y_up, to_y_dn, to_y_op = (row, y_up * NZ + z), (row, y_dn * NZ + z), (row, y_op * NZ + z)
    to_z_up, to_z_dn = (row, y * NZ + (z + 1) % NZ), (row, y * NZ + (z + NZ - 1) % NZ)
    to_x_op = (x_op * 2 + c, col)
    to_core = (x * 2 + oc, col)

    halves = (pl.ds(0, TD // 2), pl.ds(TD // 2, TD // 2))

    def at_z(d):
        return (z + NZ + d) % NZ

    used = {"send": 0, "recv": 0}
    drains = []

    def fresh(kind):
        used[kind] += 1
        return used[kind] - 1

    def group(ref, when=None):
        s = fresh("send")
        drains.append((ref, s, when))
        return s

    def remote(src, dst, to, s, sem):
        return pltpu.make_async_remote_copy(
            src_ref=src, dst_ref=dst, send_sem=send.at[s], recv_sem=sem, device_id=to, device_id_type=MESH)

    def push(src, dst, to, s, r):
        remote(src, dst, to, s, recv.at[r]).start()

    def move(view, at, to, s, r):
        push(view(at), view(at), to, s, r)

    def got(ref, r):
        remote(ref, ref, to_core, 0, recv.at[r]).wait_recv()

    class ZRing:
        def __init__(self, full, half, run):
            self.full, self.half, self.run, self.hop, self.s = full, half, run, 0, group(run(7))

        def start(self):
            s = self.hop
            up, dn = (z + NZ - s) % NZ, (z + s) % NZ
            self.r = fresh("recv")
            for at, to, h in ((up, to_z_up, 0), (dn, to_z_dn, 1)):
                move(self.full if s < 3 else lambda p: self.half(p, h), at, to, self.s, self.r)

        def advance(self):
            got(self.run(2 if self.hop < 3 else 1), self.r)
            self.hop += 1
            if self.hop < 4:
                self.start()

    class ZPair:
        def __init__(self, full, half, run):
            self.full, self.half, self.run, self.s = full, half, run, group(run(7))
            self.r = [fresh("recv") for _ in range(3)]
            for d in (2, -2, 1, -1):
                move(full, z, (row, y * NZ + at_z(d)), self.s, self.r[abs(d) - 1])

        def forward(self):
            far_up, far_dn = (row, y * NZ + at_z(2)), (row, y * NZ + at_z(-2))
            got(self.run(2), self.r[0])
            move(self.full, at_z(-1), far_up, self.s, self.r[2])
            move(self.full, at_z(1), far_dn, self.s, self.r[2])
            got(self.run(2), self.r[1])
            move(lambda p: self.half(p, 0), at_z(-2), far_up, self.s, self.r[2])
            move(lambda p: self.half(p, 1), at_z(2), far_dn, self.s, self.r[2])

        def finish(self):
            got(self.run(3), self.r[2])

    class Spread:
        def __init__(self, k, src, box, kept):
            self.k, self.box, self.kept = k, box, kept
            self.s, self.r = group(box.at[0]), fresh("recv")
            behind = (y + NY - x) % NY
            here = group(src, x != y)
            there = group(box.at[0, pl.ds(0, 3)])
            for xx in (x_op, x_up, x_dn):
                self.post(src, (xx * 2 + c, x * NZ + z), behind, there).start()

            @pl.when(x != y)
            def _():
                self.post(src, (row, x * NZ + z), behind, here).start()

            @pl.when(x == y)
            def _():
                box[c, y] = src[...]

        def post(self, src, to, behind, s):
            return remote(src, self.box.at[c, y], to, s, arrive.at[self.k, behind])

        def arrived(self):
            for behind in (1, 3, 2, 0):
                src = (y + behind) % NY
                land = self.box.at[c, src]

                def wait():
                    remote(land, land, to_core, 0, arrive.at[self.k, behind]).wait_recv()

                if behind:
                    wait()
                else:
                    pl.when(x != y)(wait)
                push(land, land, to_core, self.s, self.r)

        def keep(self, cc):
            for src in range(NY):
                hi, lo = split(self.box[cc, src])
                self.kept[cc, 0, src] = hi
                self.kept[cc, 1, src] = lo

        def finish(self):
            self.keep(c)
            got(self.box.at[0], self.r)
            self.keep(oc)

    def partial(kept, weight):
        rows = kept.shape[-2]
        total = jnp.zeros((NY * rows, MD), F32)
        for cc in range(2):
            hi = kept[cc, 0].reshape(NY * rows, MD)
            lo = kept[cc, 1].reshape(NY * rows, MD)
            total = total + dot3(hi, lo, weight(cc).reshape(MD, MD))
        return total.reshape(NY, rows, MD)

    def panel(j, k):
        return lambda cc: pt[j, k, 4 * cc:4 * cc + 4]

    class YSum:
        def __init__(self, mine, theirs, span=slice(None)):
            self.mine, self.theirs, self.span, self.r = mine, theirs, span, fresh("recv")
            s = group(theirs.at[:, span])
            for n, (yy, to) in enumerate(((y_op, to_y_op), (y_up, to_y_up), (y_dn, to_y_dn))):
                push(mine.at[yy, span], theirs.at[n, span], to, s, self.r)

        def total(self):
            mine, theirs, span = self.mine, self.theirs, self.span
            got(theirs.at[:, span], self.r)
            return (mine[y, span] + theirs[0, span]) + (theirs[1, span] + theirs[2, span])

    class YRelay:
        def __init__(self, j, h):
            self.j, self.h, self.s = j, h, group(rs.at[j, :, halves[h]])
            self.r = [fresh("recv") for _ in range(2)]
            self.via, self.to = ((y_up, to_y_up), (y_dn, to_y_dn))[h]
            other, to_other = ((y_dn, to_y_dn), (y_up, to_y_up))[h]
            push(part.at[j, y_op, halves[h]], rs.at[j, 2, halves[h]], self.to, self.s, self.r[0])
            self.pass_on(1 - h, other, to_other)

        def pass_on(self, way, yy, to):
            half = halves[self.h]
            push(part.at[self.j, yy, half], rs.at[self.j, way, half], to, self.s, self.r[1])

        def forward(self):
            j, half = self.j, halves[self.h]
            got(rs.at[j, 2, half], self.r[0])
            part[j, self.via, half] = part[j, self.via, half] + rs[j, 2, half]
            self.pass_on(self.h, self.via, self.to)

        def finish(self):
            got(rs.at[self.j, pl.ds(0, 2), halves[self.h]], self.r[1])

    def store(j):
        rows = pl.ds(j * MD, MD)
        trail[rows] = rhs_v[rows] - (part[j, y] + (rs[j, 0] + rs[j, 1])).T

    def first_part(j):
        part[j] = partial(kept(1), panel(j, 0))

    def second_part(j, h):
        part[j, :, halves[h]] = part[j, :, halves[h]] + partial(shh.at[h], panel(j, 1))
        return YRelay(j, h)

    local = []

    def bring(src, dst):
        copy = pltpu.make_async_copy(src, dst, loc.at[len(local)])
        local.append(copy)
        copy.start()

    bring(top_h, top_v)
    bring(inv_h.at[0], az.at[0, z])
    bring(cpl_h, xc)
    bring(inv_h.at[1], az.at[2, z])
    for j in range(CHUNKS):
        bring(pan_h.at[:, :, pl.ds(j * MD, MD)], pt.at[j, :, z])
    bring(rhs_h, rhs_v)

    barrier = pltpu.get_barrier_semaphore()
    peers = [(((x + dx) % NX) * 2 + c, ((y + dy) % NY) * NZ + z) for dx in range(NX) for dy in range(NY) if dx or dy]
    peers += [(row, y * NZ + at_z(d)) for d in range(1, NZ)] + [to_core]
    for peer in peers:
        pl.semaphore_signal(barrier, inc=1, device_id=peer, device_id_type=MESH)
    local[0].wait()
    xs[0] = top_v[0].T
    xs[2] = top_v[1].T
    for copy in local[1:4]:
        copy.wait()
    pl.semaphore_wait(barrier, len(peers))

    views = lambda i: (lambda p: az.at[i, p], lambda p, h: az.at[i, p, pl.ds(h * KH, KH)],
                       lambda n: az.at[i, pl.ds(0, n)])
    rings = [ZRing(lambda p, j=j: pt.at[j, :, p], lambda p, h, j=j: pt.at[j, :, p, pl.ds(h * KH, KH)],
                   lambda n, j=j: pt.at[j, :, pl.ds(0, n)]) for j in range(CHUNKS)]
    factor = lambda i: lambda cc: az[i, 4 * cc:4 * cc + 4]
    kept = lambda k: sh.at[k]
    spread = lambda k: Spread(k, xs.at[k], sb.at[k], sh.at[k])

    spread_c = Spread(4, xc, cb, ch)
    pair_a = ZPair(*views(2))
    ring_0 = ZRing(*views(0))
    ring_0.start()
    spread0 = spread(0)
    spread2 = spread(2)
    pair_a.forward()
    ring_0.advance()
    for copy in local[4:]:
        copy.wait()
    rings[0].start()
    spread_c.arrived()
    spread0.arrived()
    spread_c.finish()
    ring_0.advance()
    rings[1].start()
    pair_a.finish()
    wp[...] = partial(ch, factor(2))
    sum_w = YSum(wp, wr)
    spread0.finish()
    spread2.arrived()
    ring_0.advance()
    spread2.finish()
    az[1, z] = sum_w.total()
    pair_w = ZPair(*views(1))
    ring_0.advance()
    part[4] = partial(kept(0), factor(0))
    sum_f = YSum(part.at[4], rs.at[4])
    rings[0].advance()
    rings[2].start()
    part[5] = partial(kept(2), factor(2))
    pair_w.forward()
    first = sum_f.total()
    xs[1] = first
    spread1 = spread(1)
    solved[0] = first.T
    rings[0].advance()
    rings[1].advance()
    rings[3].start()
    spread1.arrived()
    pair_w.finish()
    spread1.finish()
    part[5] = part[5] - partial(kept(1), factor(1))
    sums_s = [YSum(part.at[5], rs.at[5], half) for half in halves]
    rings[0].advance()
    rings[1].advance()
    rings[2].advance()
    rings[3].advance()
    spreads3 = []
    for h in range(2):
        xs[3, halves[h]] = sums_s[h].total()
        spreads3.append(Spread((3, 5)[h], xs.at[3, halves[h]], sbh.at[h], shh.at[h]))
    solved[1] = xs[3].T
    rings[0].advance()
    rings[1].advance()
    first_part(0)
    rings[2].advance()
    spreads3[0].arrived()
    spreads3[0].finish()
    relays = [second_part(0, 0)]
    spreads3[1].arrived()
    rings[3].advance()
    rings[1].advance()
    spreads3[1].finish()
    relays.append(second_part(0, 1))
    first_part(1)
    relays.append(second_part(1, 0))
    rings[2].advance()
    relays[0].forward()
    relays.append(second_part(1, 1))
    rings[3].advance()
    relays[1].forward()
    rings[2].advance()
    first_part(2)
    relays[2].forward()
    relays.append(second_part(2, 0))
    relays.append(second_part(2, 1))
    relays[3].forward()
    rings[3].advance()
    first_part(3)
    relays.append(second_part(3, 0))
    relays.append(second_part(3, 1))
    for relay in relays[4:]:
        relay.forward()
    for relay in relays[:4]:
        relay.finish()
    store(0)
    store(1)
    for relay in relays[4:6]:
        relay.finish()
    store(2)
    for relay in relays[6:]:
        relay.finish()
    store(3)
    for ref, i, when in drains:
        wait = remote(ref, ref, to_core, i, recv.at[0]).wait_send
        if when is None:
            wait()
        else:
            pl.when(when)(wait)
    assert (used["send"], used["recv"], len(local)) == (N_SEND, N_RECV, N_LOCAL), used


def body(inv_diag, coupling, top_rhs, panel, rhs):
    hbm = pl.BlockSpec(memory_space=pltpu.HBM)
    vmem = pl.BlockSpec(memory_space=pltpu.VMEM)
    operands = (jnp.swapaxes(inv_diag, 1, 2), coupling.T, top_rhs, jnp.swapaxes(panel, 1, 2), rhs)
    solved, trailing = pl.pallas_call(
        kernel,
        out_shape=(jax.ShapeDtypeStruct((2, MD, TD), F32), jax.ShapeDtypeStruct((CHUNKS * MD, TD), F32)),
        in_specs=[hbm] * 5,
        out_specs=(vmem, vmem),
        scratch_shapes=[
            pltpu.VMEM((3, NZ, KD, MD), F32),
            pltpu.VMEM((CHUNKS, 2, NZ, KD, MD), F32),
            pltpu.VMEM((4, TD, MD), F32),
            pltpu.VMEM((3, 2, NY, TD, MD), F32),
            pltpu.VMEM((3, 2, 2, NY, TD, MD), BF16),
            pltpu.VMEM((2, 2, NY, TD // 2, MD), F32),
            pltpu.VMEM((2, 2, 2, NY, TD // 2, MD), BF16),
            pltpu.VMEM((2, NY, KD, MD), F32),
            pltpu.VMEM((2, 2, NY, KD, MD), BF16),
            pltpu.VMEM((KD, MD), F32),
            pltpu.VMEM((CHUNKS + 2, NY, TD, MD), F32),
            pltpu.VMEM((CHUNKS + 2, NY - 1, TD, MD), F32),
            pltpu.VMEM((NY, KD, MD), F32),
            pltpu.VMEM((NY - 1, KD, MD), F32),
            pltpu.VMEM((2, MD, TD), F32),
            pltpu.VMEM((CHUNKS * MD, TD), F32),
            pltpu.SemaphoreType.DMA((N_SEND,)),
            pltpu.SemaphoreType.DMA((N_RECV,)),
            pltpu.SemaphoreType.DMA((6, NY)),
            pltpu.SemaphoreType.DMA((N_LOCAL,)),
        ],
        compiler_params=pltpu.CompilerParams(
            collective_id=0, has_side_effects=True, vmem_limit_bytes=32 * 1024 * 1024),
    )(*(pltpu.with_memory_space_constraint(v, pltpu.HBM) for v in operands))
    return solved, trailing


def solution(mesh):
    in_specs = (
        P(None, "row", "col"),
        P("row", "col"),
        P(None, "row", "col"),
        P(None, "row", "col"),
        P("row", "col"),
    )
    out_specs = (P(None, "row", "col"), P("row", "col"))
    return jax.shard_map(body, mesh=mesh, in_specs=in_specs, out_specs=out_specs, check_vma=False)
```
